32 devices in a mesh: section: 2 (over core), dp: 4 (over y, x), tensor: 4 (over z).
Axes of the slice: x: 2, y: 2, z: 4, core: 2. Of those that a mesh axis runs over, the one named last changes fastest.
Arguments:
- section_input: bfloat16 [2, 512, 4096], P('section', 'dp'), may hold values from -60 to 60
- weights: bfloat16 [2, 4096, 4096], P('section', 'tensor', 'dp'), may hold values from -0.1875 to 0.1875
- gains: float32 [2, 4096], P('section'), may hold values from 0.1 to 1.9
- proj_seeds: int32 [2, 2], P('section'), may hold values from 0 to 99999
- out_grad: bfloat16 [512, 4096], P('dp'), may hold values from -0.75 to 0.75
- query_grads: bfloat16 [2, 256, 4096], P('section', 'dp', 'tensor'), may hold values from -0.017944336 to 0.017944336
Outputs:
- projected_grads: float32 [2, 2, 4096], P('section', None, 'tensor')
- scores: float32 [2, 256], P(None, 'dp')
The draws below stay inside these ranges and needn't reach their ends.
All inputs are finite; a program needn't handle non-finite values.
Results may differ from the reference program's by a relative error of at most 0.033.
Values may be sent and summed in bfloat16 or wider, within the bound.
A program may use at most 64 MiB of HBM per device.

```python
import math
import jax
import jax.numpy as jnp
from jax import lax

D = 4096
R = 64
SEQS = 2
LAYERS = 2
TOKENS = 512
SEQ_LEN = 256
QUERIES = 256
N_TENSOR = 4


def draw_section_input(key, part):
    key_values = jax.random.fold_in(key, 101)
    key_columns = jax.random.fold_in(key, 202)
    key_rows = jax.random.fold_in(key, 303)
    col_scale = jnp.exp(jax.random.uniform(key_columns, (LAYERS, 1, D), jnp.float32, 0.0, math.log(10.0)))
    row_scale = jnp.exp(jax.random.uniform(key_rows, (LAYERS, TOKENS, 1), jnp.float32, 0.0, math.log(3.0)))
    values = jax.random.normal(key_values, (LAYERS, TOKENS, D), jnp.float32) * col_scale
    values = values * row_scale
    return jnp.clip(values, -60.0, 60.0).astype(jnp.bfloat16)


def place_ends(entries, stream_key, low, top_value):
    extent = entries.shape
    place = [jax.random.randint(jax.random.fold_in(stream_key, axis), (), 0, extent[axis]) for axis in range(len(extent))]
    entries = entries.at[tuple(place)].set(low)
    longest = extent.index(max(extent))
    place[longest] = (place[longest] + 1) % extent[longest]
    return entries.at[tuple(place)].set(top_value)


def steps_of(rng, extent, shards, low, high):
    factor_of, own = 1.0, jax.random.fold_in(rng, 6)
    for axis_at, shards_of in shards:
        steps = jnp.exp(jax.random.uniform(jax.random.fold_in(own, axis_at), (shards_of,), jnp.float32, low / len(shards), high / len(shards)))
        factor_of = factor_of * jnp.repeat(steps, extent[axis_at] // shards_of).reshape([-1 if axis == axis_at else 1 for axis in range(len(extent))])
    return factor_of


def gaussian(own_key, shape, spread, reach, pieces=(), kind=jnp.bfloat16):
    factor_of = steps_of(own_key, shape, pieces, -0.22, 0.18) if pieces else 1.0
    array = jax.random.normal(own_key, shape, jnp.float32) * spread * factor_of
    return jnp.minimum(jnp.maximum(array, -reach), reach).astype(kind)


def setup_inputs(seed: int = 0) -> dict:
    streams_of = jax.random.split(jax.random.key(seed), 7)
    return {
        "section_input": draw_section_input(jax.random.fold_in(streams_of[6], 71), 0),
        "weights": gaussian(streams_of[1], (LAYERS, D, D), (D // 4) ** -0.5, 0.1875, ((0, 2), (1, 4), (2, 4))),
        "gains": jnp.clip(1.0 + 0.18 * jax.random.normal(streams_of[2], (LAYERS, D), jnp.float32), 0.1, 1.9),
        "proj_seeds": place_ends(jax.random.randint(streams_of[3], (LAYERS, 2), 0, 100000), jax.random.fold_in(streams_of[3], 1), 0, 99999).astype(jnp.int32),
        "out_grad": gaussian(streams_of[4], (TOKENS, D), 0.125, 0.75, ((0, 4),)),
        "query_grads": gaussian(streams_of[5], (LAYERS, QUERIES, R * R), 0.003, 0.017944336, ((0, 2), (1, 4), (2, 4))),
    }


eps = 1e-05

def sign_table(seed_value, row_count):
    row_index = lax.broadcasted_iota(jnp.int32, (row_count, R), 0)
    col_index = lax.broadcasted_iota(jnp.int32, (row_count, R), 1)
    mixing = row_index * 40503 + col_index * 9973 + seed_value.astype(jnp.int32) * 7919 + 12345
    mixing = mixing ^ mixing >> 13
    mixing = mixing * 1274126177
    mixing = mixing ^ mixing >> 16
    parity = mixing >> 10 & 1
    return (jnp.where(parity == 1, 1.0, -1.0) * (1.0 / math.sqrt(row_count))).astype(jnp.bfloat16)

def silu_slope(values):
    sigmoid_v = jax.nn.sigmoid(values)
    return sigmoid_v * (1.0 + values * (1.0 - sigmoid_v))

def reference(section_input, weights, gains, proj_seeds, out_grad, query_grads):

    def layer_step(upstream, layer):
        layer_input, weight, gain_row, seed_pair, queries = layer
        hidden_in = layer_input.astype(jnp.float32)
        radius = jnp.sqrt(lax.optimization_barrier(jnp.mean(hidden_in * hidden_in, axis=1, keepdims=True)) + eps)
        normed = hidden_in / radius
        lifted = (normed * gain_row).astype(jnp.bfloat16)
        block_width = D // N_TENSOR
        summed = jnp.zeros((TOKENS, D), jnp.float32)
        for part_index in range(N_TENSOR):
            low_col = part_index * block_width
            partial_value = jnp.dot(lifted[:, low_col:low_col + block_width], weight[low_col:low_col + block_width, :], preferred_element_type=jnp.float32)
            summed = summed + lax.optimization_barrier(partial_value.astype(jnp.bfloat16)).astype(jnp.float32)
        proj_in = sign_table(seed_pair[0], D)
        proj_out = sign_table(seed_pair[1], D)
        in_features = jnp.dot(lifted, proj_in, preferred_element_type=jnp.float32).astype(jnp.bfloat16)
        grad_pre = (upstream.astype(jnp.float32) * silu_slope(summed)).astype(jnp.bfloat16)
        out_features = jnp.dot(grad_pre, proj_out, preferred_element_type=jnp.float32).astype(jnp.bfloat16)
        grad_norm = jnp.dot(grad_pre, weight.T, preferred_element_type=jnp.float32).astype(jnp.bfloat16)
        scaled = grad_norm.astype(jnp.float32) * gain_row
        mean_dot = lax.optimization_barrier(jnp.mean(scaled * normed, axis=1, keepdims=True))
        downstream = (upstream.astype(jnp.float32) + (scaled - normed * mean_dot) / radius).astype(jnp.bfloat16)
        left = in_features.astype(jnp.float32).reshape(SEQS, SEQ_LEN, R)
        right = out_features.astype(jnp.float32).reshape(SEQS, SEQ_LEN, R)
        grads = jnp.einsum('kti,ktj->kij', left, right, precision=lax.Precision.HIGHEST).reshape(SEQS, R * R)
        score_part = jnp.dot(grads, queries.astype(jnp.float32).T, precision=lax.Precision.HIGHEST)
        return (downstream, (grads, score_part))
    final_grad, outputs = lax.scan(layer_step, out_grad, (section_input, weights, gains, proj_seeds, query_grads), reverse=True)
    projected_grads, score_parts = outputs
    return (projected_grads, lax.optimization_barrier(jnp.sum(score_parts, axis=0)))
```

```python
import functools
import math

import jax
import jax.numpy as jnp
from jax import lax
from jax.experimental import pallas as pl
from jax.experimental.pallas import tpu as pltpu
from jax.sharding import PartitionSpec as P

R = 64
SEQS = 2
eps = 1e-05
F32 = jnp.float32
BF16 = jnp.bfloat16
MESH = pl.DeviceIdType.MESH
NT = (((1,), (1,)), ((), ()))


def sign_rows(seed_value, row_start, row_count, scale):
    row_index = lax.broadcasted_iota(jnp.int32, (R, row_count), 1) + row_start
    col_index = lax.broadcasted_iota(jnp.int32, (R, row_count), 0)
    mixing = row_index * 40503 + col_index * 9973 + (seed_value * 7919 + 12345)
    mixing = mixing ^ (mixing >> 13)
    mixing = mixing * 1274126177
    mixing = mixing ^ (mixing >> 16)
    parity = (mixing >> 10) & 1
    return jnp.where(parity == 1, scale, -scale).astype(BF16)


def kernel(
    sections, nd, nz,
    x_ref, w_ref, gain_ref, seed_ref, og_ref, q_ref,
    grads_ref, scores_ref,
    a_buf, inf_buf, ps_buf, pr_buf, slope_buf, ui_buf, uii_buf, gp_buf,
    gns_buf, gnr_buf, dot_buf, up_buf, g_buf, gr_buf, sc_buf,
    a_ss, a_rs, inf_ss, inf_rs, p_ss, p_rs, og_ss, og_rs, gp_ss, gp_rs,
    gn_ss, gn_rs, dt_ss, dt_rs, up_ss, up_rs, uii_ss, uii_rs,
    g_ss, g_rs, sc_ss, sc_rs,
):
    s = lax.axis_index("section")
    d = lax.axis_index("dp")
    z = lax.axis_index("tensor")
    tok, width = x_ref.shape
    feat = width // nz
    cols = width // nd
    sub = tok // nz
    at_top = s == sections - 1
    lower = s > 0
    z_start = pl.multiple_of(z * feat, feat)
    d_start = pl.multiple_of(d * cols, cols)
    sub_start = pl.multiple_of(z * sub, sub)

    def dev(s_to, d_to, z_to):
        return {"section": s_to, "dp": d_to, "tensor": z_to}

    def remote(src, dst, ss, rs, to):
        return pltpu.make_async_remote_copy(
            src_ref=src, dst_ref=dst, send_sem=ss, recv_sem=rs, device_id=to, device_id_type=MESH
        )

    barrier = pltpu.get_barrier_semaphore()
    total = sections * nd * nz
    me = (s * nd + d) * nz + z

    @pl.loop(1, total)
    def _(step):
        other = lax.rem(me + step, total)
        pl.semaphore_signal(
            barrier, inc=1, device_id_type=MESH,
            device_id=dev(other // (nd * nz), lax.rem(other // nz, nd), lax.rem(other, nz)),
        )

    hidden = x_ref[...].astype(F32)
    radius = jnp.sqrt(jnp.mean(hidden * hidden, axis=1, keepdims=True) + eps)
    gain_z = gain_ref[:, pl.ds(z_start, feat)]
    normed_z = x_ref[:, pl.ds(z_start, feat)].astype(F32) / radius
    a_buf[d] = (normed_z * gain_z).astype(BF16)

    pl.semaphore_wait(barrier, total - 1)

    def a_copy(o):
        to = lax.rem(d + o, nd)
        return remote(a_buf.at[d], a_buf.at[d], a_ss.at[o], a_rs.at[o], dev(s, to, z))

    for o in range(1, nd):
        a_copy(o).start()

    def og_copy(o):
        to = lax.rem(d + o, nd)
        src = og_ref.at[pl.ds(sub_start, sub), pl.ds(pl.multiple_of(to * cols, cols), cols)]
        return remote(src, ui_buf.at[d], og_ss.at[o], og_rs.at[o], dev(s, to, z))

    @pl.when(at_top)
    def _():
        for o in range(1, nd):
            og_copy(o).start()
        ui_buf[d] = og_ref[pl.ds(sub_start, sub), pl.ds(d_start, cols)]

    scale = 1.0 / math.sqrt(width)
    x_sub = x_ref[pl.ds(sub_start, sub), :].astype(F32)
    radius_sub = jnp.sqrt(jnp.mean(x_sub * x_sub, axis=1, keepdims=True) + eps)
    lifted_sub = (x_sub / radius_sub * gain_ref[...]).astype(BF16)
    table_in = sign_rows(seed_ref[0, 0], 0, width, scale)
    inf_buf[d] = lax.dot_general(lifted_sub, table_in, NT, preferred_element_type=F32)

    def inf_copy(o):
        to = lax.rem(d + o, nd)
        return remote(inf_buf.at[d], inf_buf.at[d], inf_ss.at[o], inf_rs.at[o], dev(s, to, z))

    for o in range(1, nd):
        inf_copy(o).start()

    for o in range(nd):
        block = lax.rem(d + nd - o, nd)
        if o:
            a_copy(o).wait_recv()
        part = jnp.dot(a_buf[block], w_ref[...], preferred_element_type=F32).astype(BF16)
        for zt in range(nz):
            ps_buf[zt, block] = part[zt * sub : (zt + 1) * sub, :]

    def p_copy(o):
        to = lax.rem(z + o, nz)
        return remote(ps_buf.at[to], pr_buf.at[z], p_ss.at[o], p_rs.at[o], dev(s, d, to))

    for o in range(1, nz):
        p_copy(o).start()
    pr_buf[z] = ps_buf[z]
    table_out = sign_rows(seed_ref[0, 1], d_start, cols, scale)
    for o in range(1, nz):
        p_copy(o).wait_recv()
    summed = pr_buf[0].astype(F32)
    for zt in range(1, nz):
        summed = summed + pr_buf[zt].astype(F32)
    sig = jax.nn.sigmoid(summed)
    slope_buf[...] = sig * (1.0 + summed * (1.0 - sig))

    def up_copy(zt, source):
        return remote(
            up_buf.at[pl.ds(zt * sub, sub)], ui_buf.at[source], up_ss.at[zt], up_rs.at[source],
            dev(jnp.maximum(s - 1, 0), z, zt),
        )

    def uii_copy():
        return remote(up_buf, uii_buf, uii_ss.at[0], uii_rs.at[0], dev(jnp.maximum(s - 1, 0), d, z))

    @pl.when(at_top)
    def _():
        for o in range(1, nd):
            og_copy(o).wait_recv()
        uii_buf[...] = og_ref[:, pl.ds(z_start, feat)]

    @pl.when(jnp.logical_not(at_top))
    def _():
        for source in range(nd):
            up_copy(0, source).wait_recv()

    grad_pre = (ui_buf[...].astype(F32) * slope_buf[...]).astype(BF16)
    gp_buf[z] = grad_pre

    def gp_copy(o):
        to = lax.rem(z + o, nz)
        return remote(gp_buf.at[z], gp_buf.at[z], gp_ss.at[o], gp_rs.at[o], dev(s, d, to))

    @pl.when(lower)
    def _():
        for o in range(1, nz):
            gp_copy(o).start()

    for o in range(1, nd):
        inf_copy(o).wait_recv()
    out_feat = lax.dot_general(
        grad_pre.reshape(nd * sub, cols), table_out, NT, preferred_element_type=F32
    ).astype(BF16)
    in_feat = inf_buf[...].reshape(nd * sub, R).astype(BF16)
    piece = R * R // nz
    per_seq = nd * sub // SEQS
    for zt in range(nz):
        entry = lax.broadcasted_iota(jnp.int32, (R, piece), 1) + zt * piece
        which = lax.broadcasted_iota(jnp.int32, (R, piece), 0)
        pick_in = (entry // R == which).astype(F32).astype(BF16)
        pick_out = (entry % R == which).astype(F32).astype(BF16)
        left = jnp.dot(in_feat, pick_in, preferred_element_type=F32)
        right = jnp.dot(out_feat, pick_out, preferred_element_type=F32)
        product = left * right
        for k in range(SEQS):
            g_buf[zt, k : k + 1, :] = jnp.sum(
                product[k * per_seq : (k + 1) * per_seq], axis=0, keepdims=True
            )

    plane = nd * nz
    mine = d * nz + z

    def g_copy(o):
        to = lax.rem(mine + o, plane)
        return remote(
            g_buf.at[lax.rem(to, nz)], gr_buf.at[mine], g_ss.at[o], g_rs.at[o],
            dev(s, to // nz, lax.rem(to, nz)),
        )

    for o in range(1, plane):
        g_copy(o).start()
    gr_buf[mine] = g_buf[z]

    def gn_copy(o):
        to = lax.rem(d + o, nd)
        return remote(gns_buf.at[to], gnr_buf.at[d], gn_ss.at[o], gn_rs.at[o], dev(s, to, z))

    def dt_copy(o):
        to = lax.rem(z + o, nz)
        return remote(dot_buf.at[z], dot_buf.at[z], dt_ss.at[o], dt_rs.at[o], dev(s, d, to))

    @pl.when(lower)
    def _():
        for o in range(nz):
            block = lax.rem(z + nz - o, nz)
            if o:
                gp_copy(o).wait_recv()
            rows = gp_buf[block].reshape(nd * sub, cols)
            part = lax.dot_general(rows, w_ref[...], NT, preferred_element_type=F32).astype(BF16)
            for dt in range(nd):
                gns_buf[dt, block] = part[dt * sub : (dt + 1) * sub, :]
        for o in range(1, nd):
            gn_copy(o).start()
        gnr_buf[d] = gns_buf[d]
        for o in range(1, nd):
            gn_copy(o).wait_recv()
        grad_norm = gnr_buf[0].astype(F32)
        for dt in range(1, nd):
            grad_norm = grad_norm + gnr_buf[dt].astype(F32)
        grad_norm = grad_norm.astype(BF16).astype(F32).reshape(tok, feat)
        scaled = grad_norm * gain_ref[:, pl.ds(z_start, feat)]
        x_z = x_ref[:, pl.ds(z_start, feat)].astype(F32)
        x_all = x_ref[...].astype(F32)
        rad = jnp.sqrt(jnp.mean(x_all * x_all, axis=1, keepdims=True) + eps)
        normed = x_z / rad
        own_dot = jnp.sum(scaled * normed, axis=1, keepdims=True)
        dot_buf[z] = jnp.broadcast_to(own_dot, (tok, tok)).T[:8, :]
        for o in range(1, nz):
            dt_copy(o).start()
        if sections > 2:
            @pl.when(jnp.logical_not(at_top))
            def _():
                uii_copy().wait_recv()
        for o in range(1, nz):
            dt_copy(o).wait_recv()
        dots = dot_buf[0]
        for zt in range(1, nz):
            dots = dots + dot_buf[zt]
        mean_dot = jnp.broadcast_to(dots[:1, :], (tok, tok)).T[:, :1] * (1.0 / width)
        up_buf[...] = (uii_buf[...].astype(F32) + (scaled - normed * mean_dot) / rad).astype(BF16)
        for zt in range(nz):
            up_copy(zt, d).start()
        if sections > 2:
            @pl.when(s > 1)
            def _():
                uii_copy().start()

    for o in range(1, plane):
        g_copy(o).wait_recv()
    grads = gr_buf[0]
    for other in range(1, plane):
        grads = grads + gr_buf[other]
    grads_ref[...] = grads
    queries = q_ref[...]
    high = grads.astype(BF16)
    rest = grads - high.astype(F32)
    middle = rest.astype(BF16)
    low = (rest - middle.astype(F32)).astype(BF16)
    part = lax.dot_general(high, queries, NT, preferred_element_type=F32)
    part = part + lax.dot_general(middle, queries, NT, preferred_element_type=F32)
    part = part + lax.dot_general(low, queries, NT, preferred_element_type=F32)
    column = sections * nz
    here = s * nz + z
    sc_buf[here] = part

    def sc_copy(o):
        to = lax.rem(here + o, column)
        return remote(
            sc_buf.at[here], sc_buf.at[here], sc_ss.at[o], sc_rs.at[o],
            dev(to // nz, d, lax.rem(to, nz)),
        )

    for o in range(1, column):
        sc_copy(o).start()

    for o in range(1, nd):
        a_copy(o).wait_send()
        inf_copy(o).wait_send()
    for o in range(1, nz):
        p_copy(o).wait_send()

    @pl.when(at_top)
    def _():
        for o in range(1, nd):
            og_copy(o).wait_send()

    @pl.when(lower)
    def _():
        for o in range(1, nz):
            gp_copy(o).wait_send()
            dt_copy(o).wait_send()
        for o in range(1, nd):
            gn_copy(o).wait_send()
        for zt in range(nz):
            up_copy(zt, d).wait_send()
        if sections > 2:
            @pl.when(s > 1)
            def _():
                uii_copy().wait_send()

    for o in range(1, plane):
        g_copy(o).wait_send()
    for o in range(1, column):
        sc_copy(o).wait_recv()
    scores = sc_buf[0]
    for other in range(1, column):
        scores = scores + sc_buf[other]
    scores_ref[...] = scores
    for o in range(1, column):
        sc_copy(o).wait_send()


def body(section_input, weights, gains, proj_seeds, out_grad, query_grads):
    sections = lax.axis_size("section")
    nd = lax.axis_size("dp")
    nz = lax.axis_size("tensor")
    tok, width = section_input.shape[1:]
    feat = weights.shape[1]
    cols = weights.shape[2]
    assert nd == nz and feat == cols
    sub = tok // nz
    piece = R * R // nz
    queries = query_grads.shape[1]
    column = sections * nz
    plane = nd * nz
    vmem = pl.BlockSpec(memory_space=pltpu.VMEM)
    dma = pltpu.SemaphoreType.DMA
    sems = []
    for count in (nd, nd, nz, nd, nz, nd, nz):
        sems += [dma((count,)), dma((count,))]
    sems += [dma((nz,)), dma((nd,)), dma((1,)), dma((1,))]
    sems += [dma((plane,)), dma((plane,)), dma((column,)), dma((column,))]
    grads, scores = pl.pallas_call(
        functools.partial(kernel, sections, nd, nz),
        out_shape=(
            jax.ShapeDtypeStruct((SEQS, piece), F32),
            jax.ShapeDtypeStruct((SEQS, queries), F32),
        ),
        in_specs=[vmem, vmem, vmem, pl.BlockSpec(memory_space=pltpu.SMEM), vmem, vmem],
        out_specs=(vmem, vmem),
        scratch_shapes=[
            pltpu.VMEM((nd, tok, feat), BF16),
            pltpu.VMEM((nd, sub, R), F32),
            pltpu.VMEM((nz, nd, sub, cols), BF16),
            pltpu.VMEM((nz, nd, sub, cols), BF16),
            pltpu.VMEM((nd, sub, cols), F32),
            pltpu.VMEM((nd, sub, cols), BF16),
            pltpu.VMEM((tok, feat), BF16),
            pltpu.VMEM((nz, nd, sub, cols), BF16),
            pltpu.VMEM((nd, nz, sub, feat), BF16),
            pltpu.VMEM((nd, nz, sub, feat), BF16),
            pltpu.VMEM((nz, 8, tok), F32),
            pltpu.VMEM((tok, feat), BF16),
            pltpu.VMEM((nz, SEQS, piece), F32),
            pltpu.VMEM((plane, SEQS, piece), F32),
            pltpu.VMEM((column, SEQS, queries), F32),
            *sems,
        ],
        compiler_params=pltpu.CompilerParams(
            collective_id=0, has_side_effects=True, vmem_limit_bytes=60 * 1024 * 1024
        ),
    )(section_input[0], weights[0], gains, proj_seeds, out_grad, query_grads[0])
    return (grads[None], scores)


def solution(mesh):
    in_specs = (
        P("section", "dp", None),
        P("section", "tensor", "dp"),
        P("section", None),
        P("section", None),
        P("dp", None),
        P("section", "dp", "tensor"),
    )
    out_specs = (P("section", None, "tensor"), P(None, "dp"))
    return jax.shard_map(body, mesh=mesh, in_specs=in_specs, out_specs=out_specs, check_vma=False)
```

```python
import functools
import math

import jax
import jax.numpy as jnp
from jax import lax
from jax.experimental import pallas as pl
from jax.experimental.pallas import tpu as pltpu
from jax.sharding import PartitionSpec as P

R = 64
SEQS = 2
eps = 1e-05
F32 = jnp.float32
BF16 = jnp.bfloat16
MESH = pl.DeviceIdType.MESH
NT = (((1,), (1,)), ((), ()))


def sign_rows(seed_value, row_start, row_count, scale):
    row_index = lax.broadcasted_iota(jnp.int32, (R, row_count), 1) + row_start
    col_index = lax.broadcasted_iota(jnp.int32, (R, row_count), 0)
    mixing = row_index * 40503 + col_index * 9973 + (seed_value * 7919 + 12345)
    mixing = mixing ^ (mixing >> 13)
    mixing = mixing * 1274126177
    mixing = mixing ^ (mixing >> 16)
    parity = (mixing >> 10) & 1
    return jnp.where(parity == 1, scale, -scale).astype(BF16)


def kernel(
    sections, nd, nz,
    x_hbm, w_hbm, gain_ref, seed_ref, og_ref, q_ref,
    grads_ref, scores_ref,
    a_buf, inf_buf, ps_buf, pr_buf, slope_buf, ui_buf, uii_buf, gp_buf,
    gns_buf, gnr_buf, dot_buf, up_buf, g_buf, gr_buf, sc_buf,
    x_ref, w_ref, sum_buf, norm_buf, rad_buf, turn_buf, mean_buf,
    a_ss, a_rs, inf_ss, inf_rs, p_ss, p_rs, og_ss, og_rs, gp_ss, gp_rs,
    gn_ss, gn_rs, dt_ss, dt_rs, up_ss, up_rs, uii_ss, uii_rs,
    g_ss, g_rs, sc_ss, sc_rs, in_sem, go_sem,
):
    s = lax.axis_index("section")
    d = lax.axis_index("dp")
    z = lax.axis_index("tensor")
    tok, width = x_hbm.shape
    feat = width // nz
    cols = width // nd
    sub = tok // nz
    at_top = s == sections - 1
    below_top = s == sections - 2
    lower = s > 0
    z_start = pl.multiple_of(z * feat, feat)
    d_start = pl.multiple_of(d * cols, cols)
    sub_start = pl.multiple_of(z * sub, sub)
    sub_start_d = pl.multiple_of(d * sub, sub)

    def dev(s_to, d_to, z_to):
        return {"section": s_to, "dp": d_to, "tensor": z_to}

    def remote(src, dst, ss, rs, to):
        return pltpu.make_async_remote_copy(
            src_ref=src, dst_ref=dst, send_sem=ss, recv_sem=rs, device_id=to, device_id_type=MESH
        )

    x_load = pltpu.make_async_copy(x_hbm, x_ref, in_sem.at[0])
    w_load = pltpu.make_async_copy(w_hbm, w_ref, in_sem.at[1])
    x_load.start()
    w_load.start()

    barrier = pltpu.get_barrier_semaphore()
    total = sections * nd * nz
    me = (s * nd + d) * nz + z

    @pl.loop(1, total)
    def _(step):
        other = lax.rem(me + step, total)
        pl.semaphore_signal(
            barrier, inc=1, device_id_type=MESH,
            device_id=dev(other // (nd * nz), lax.rem(other // nz, nd), lax.rem(other, nz)),
        )

    x_load.wait()
    hidden = x_ref[...].astype(F32)
    radius = jnp.sqrt(jnp.mean(hidden * hidden, axis=1, keepdims=True) + eps)
    gain_z = gain_ref[:, pl.ds(z_start, feat)]
    normed_z = x_ref[:, pl.ds(z_start, feat)].astype(F32) / radius
    norm_buf[...] = normed_z
    rad_buf[...] = jnp.broadcast_to(radius, rad_buf.shape)
    a_buf[d] = (normed_z * gain_z).astype(BF16)

    pl.semaphore_wait(barrier, total - 1)

    def a_copy(o):
        to = lax.rem(d + o, nd)
        return remote(a_buf.at[d], a_buf.at[d], a_ss.at[o], a_rs.at[o], dev(s, to, z))

    @pl.when(jnp.logical_not(below_top))
    def _():
        for o in range(1, nd):
            a_copy(o).start()

    def og_copy(o):
        to = lax.rem(d + o, nd)
        src = og_ref.at[pl.ds(sub_start, sub), pl.ds(pl.multiple_of(to * cols, cols), cols)]
        return remote(src, ui_buf.at[d], og_ss.at[o], og_rs.at[o], dev(s, to, z))

    def ui_load():
        src = og_ref.at[pl.ds(sub_start, sub), pl.ds(d_start, cols)]
        return pltpu.make_async_copy(src, ui_buf.at[d], in_sem.at[2])

    def uii_load():
        return pltpu.make_async_copy(og_ref.at[:, pl.ds(z_start, feat)], uii_buf, in_sem.at[3])

    @pl.when(at_top)
    def _():
        for o in range(1, nd):
            og_copy(o).start()
        ui_load().start()
        uii_load().start()

    scale = 1.0 / math.sqrt(width)
    x_sub = x_ref[pl.ds(sub_start, sub), :].astype(F32)
    radius_sub = jnp.sqrt(jnp.mean(x_sub * x_sub, axis=1, keepdims=True) + eps)
    lifted_sub = (x_sub / radius_sub * gain_ref[...]).astype(BF16)
    table_in = sign_rows(seed_ref[0, 0], 0, width, scale)
    inf_buf[d] = lax.dot_general(lifted_sub, table_in, NT, preferred_element_type=F32)

    def inf_copy(o):
        to = lax.rem(d + o, nd)
        return remote(inf_buf.at[d], inf_buf.at[d], inf_ss.at[o], inf_rs.at[o], dev(s, to, z))

    for o in range(1, nd):
        inf_copy(o).start()

    @pl.when(below_top)
    def _():
        pl.semaphore_wait(go_sem.at[0], 1)
        for o in range(1, nd):
            a_copy(o).start()

    w_load.wait()
    for o in range(nd):
        block = lax.rem(d + nd - o, nd)
        if o:
            a_copy(o).wait_recv()
        part = jnp.dot(a_buf[block], w_ref[...], preferred_element_type=F32).astype(BF16)
        for zt in range(nz):
            ps_buf[zt, block] = part[zt * sub : (zt + 1) * sub, :]

    for o in range(1, nd):
        a_copy(o).wait_send()

    def go(which):
        pl.semaphore_signal(
            go_sem.at[which], inc=1, device_id=dev(jnp.maximum(s - 1, 0), d, z), device_id_type=MESH
        )

    if sections > 1:
        @pl.when(at_top)
        def _():
            go(0)

        @pl.when(below_top)
        def _():
            pl.semaphore_wait(go_sem.at[1], 1)

    def p_copy(o):
        to = lax.rem(z + o, nz)
        return remote(ps_buf.at[to], pr_buf.at[z], p_ss.at[o], p_rs.at[o], dev(s, d, to))

    for o in range(1, nz):
        p_copy(o).start()
    pr_buf[z] = ps_buf[z]
    table_out = sign_rows(seed_ref[0, 1], d_start, cols, scale)
    for o in range(1, nz):
        p_copy(o).wait_recv()
    summed = pr_buf[0].astype(F32)
    for zt in range(1, nz):
        summed = summed + pr_buf[zt].astype(F32)
    sig = jax.nn.sigmoid(summed)
    sum_buf[...] = summed
    slope_buf[...] = sig * (1.0 + summed * (1.0 - sig))

    def up_copy(zt, source):
        return remote(
            up_buf.at[pl.ds(zt * sub, sub)], ui_buf.at[source], up_ss.at[zt], up_rs.at[source],
            dev(jnp.maximum(s - 1, 0), z, zt),
        )

    def uii_copy():
        return remote(up_buf, uii_buf, uii_ss.at[0], uii_rs.at[0], dev(jnp.maximum(s - 1, 0), d, z))

    @pl.when(at_top)
    def _():
        for o in range(1, nd):
            og_copy(o).wait_recv()
        ui_load().wait()
        uii_load().wait()

    @pl.when(jnp.logical_not(at_top))
    def _():
        for source in range(nd):
            up_copy(0, source).wait_recv()

    grad_pre = (ui_buf[...].astype(F32) * slope_buf[...]).astype(BF16)
    gp_buf[z] = grad_pre

    def gp_copy(o):
        to = lax.rem(z + o, nz)
        return remote(gp_buf.at[z], gp_buf.at[z], gp_ss.at[o], gp_rs.at[o], dev(s, d, to))

    plane = nd * nz
    mine = d * nz + z

    def dt_copy(o):
        to = lax.rem(mine + o, plane)
        return remote(
            dot_buf.at[mine], dot_buf.at[mine], dt_ss.at[o], dt_rs.at[o],
            dev(s, to // nz, lax.rem(to, nz)),
        )

    @pl.when(lower)
    def _():
        for o in range(1, nz):
            gp_copy(o).start()
        pre = gp_buf[z].astype(F32) * sum_buf[...]
        own_dot = jnp.sum(pre.reshape(nd * sub, cols), axis=1, keepdims=True)
        dot_buf[mine] = jnp.broadcast_to(own_dot, (tok, tok)).T[:8, :]
        for o in range(1, plane):
            dt_copy(o).start()

    for o in range(1, nd):
        inf_copy(o).wait_recv()
    out_feat = lax.dot_general(
        grad_pre.reshape(nd * sub, cols), table_out, NT, preferred_element_type=F32
    ).astype(BF16)
    in_feat = inf_buf[...].reshape(nd * sub, R).astype(BF16)
    piece = R * R // nz
    per_seq = nd * sub // SEQS
    for zt in range(nz):
        entry = lax.broadcasted_iota(jnp.int32, (R, piece), 1) + zt * piece
        which = lax.broadcasted_iota(jnp.int32, (R, piece), 0)
        pick_in = (entry // R == which).astype(F32).astype(BF16)
        pick_out = (entry % R == which).astype(F32).astype(BF16)
        left = jnp.dot(in_feat, pick_in, preferred_element_type=F32)
        right = jnp.dot(out_feat, pick_out, preferred_element_type=F32)
        product = left * right
        for k in range(SEQS):
            g_buf[zt, k : k + 1, :] = jnp.sum(
                product[k * per_seq : (k + 1) * per_seq], axis=0, keepdims=True
            )

    def g_copy(o):
        to = lax.rem(mine + o, plane)
        return remote(
            g_buf.at[lax.rem(to, nz)], gr_buf.at[mine], g_ss.at[o], g_rs.at[o],
            dev(s, to // nz, lax.rem(to, nz)),
        )

    for o in range(1, plane):
        g_copy(o).start()
    gr_buf[mine] = g_buf[z]

    def gn_copy(o):
        to = lax.rem(d + o, nd)
        return remote(gns_buf.at[to], gnr_buf.at[d], gn_ss.at[o], gn_rs.at[o], dev(s, to, z))

    @pl.when(lower)
    def _():
        for o in range(nz):
            block = lax.rem(z + nz - o, nz)
            if o:
                gp_copy(o).wait_recv()
            rows = gp_buf[block].reshape(nd * sub, cols)
            part = lax.dot_general(rows, w_ref[...], NT, preferred_element_type=F32).astype(BF16)
            for dt in range(nd):
                gns_buf[dt, block] = part[dt * sub : (dt + 1) * sub, :]
        for o in range(1, nz):
            gp_copy(o).wait_send()

        @pl.when(at_top)
        def _():
            go(1)

        for o in range(1, nd):
            gn_copy(o).start()
        gnr_buf[d] = gns_buf[d]
        for o in range(1, plane):
            dt_copy(o).wait_recv()
        for zt in range(nz):
            dots = dot_buf[zt]
            for dt in range(1, nd):
                dots = dots + dot_buf[dt * nz + zt]
            turn_buf[...] = jnp.broadcast_to(dots[:1, :] * (1.0 / width), (tok, tok)).T
            mean_buf[zt] = turn_buf[pl.ds(sub_start_d, sub), :]
        for o in range(1, nd):
            gn_copy(o).wait_recv()
        grad_norm = gnr_buf[0].astype(F32)
        for dt in range(1, nd):
            grad_norm = grad_norm + gnr_buf[dt].astype(F32)
        grad_norm = grad_norm.astype(BF16).astype(F32).reshape(tok, feat)
        scaled = grad_norm * gain_ref[:, pl.ds(z_start, feat)]
        normed = norm_buf[...]
        rad = rad_buf[:, :1]
        mean_dot = mean_buf[...].reshape(tok, tok)[:, :1]
        if sections > 2:
            @pl.when(jnp.logical_not(at_top))
            def _():
                uii_copy().wait_recv()
        up_buf[...] = (uii_buf[...].astype(F32) + (scaled - normed * mean_dot) / rad).astype(BF16)
        for zt in range(nz):
            up_copy(zt, d).start()
        if sections > 2:
            @pl.when(s > 1)
            def _():
                uii_copy().start()

    for o in range(1, plane):
        g_copy(o).wait_recv()
    grads = gr_buf[0]
    for other in range(1, plane):
        grads = grads + gr_buf[other]
    grads_ref[...] = grads
    queries = q_ref[...]
    high = grads.astype(BF16)
    rest = grads - high.astype(F32)
    middle = rest.astype(BF16)
    low = (rest - middle.astype(F32)).astype(BF16)
    part = lax.dot_general(high, queries, NT, preferred_element_type=F32)
    part = part + lax.dot_general(middle, queries, NT, preferred_element_type=F32)
    part = part + lax.dot_general(low, queries, NT, preferred_element_type=F32)
    column = sections * nz
    here = s * nz + z
    sc_buf[here] = part

    def sc_copy(o):
        to = lax.rem(here + o, column)
        return remote(
            sc_buf.at[here], sc_buf.at[here], sc_ss.at[o], sc_rs.at[o],
            dev(to // nz, d, lax.rem(to, nz)),
        )

    for o in range(1, column):
        sc_copy(o).start()

    for o in range(1, nd):
        inf_copy(o).wait_send()
    for o in range(1, nz):
        p_copy(o).wait_send()

    @pl.when(at_top)
    def _():
        for o in range(1, nd):
            og_copy(o).wait_send()

    @pl.when(lower)
    def _():
        for o in range(1, plane):
            dt_copy(o).wait_send()
        for o in range(1, nd):
            gn_copy(o).wait_send()
        for zt in range(nz):
            up_copy(zt, d).wait_send()
        if sections > 2:
            @pl.when(s > 1)
            def _():
                uii_copy().wait_send()

    for o in range(1, plane):
        g_copy(o).wait_send()
    for o in range(1, column):
        sc_copy(o).wait_recv()
    scores = sc_buf[0]
    for other in range(1, column):
        scores = scores + sc_buf[other]
    scores_ref[...] = scores
    for o in range(1, column):
        sc_copy(o).wait_send()


def body(section_input, weights, gains, proj_seeds, out_grad, query_grads):
    sections = lax.axis_size("section")
    nd = lax.axis_size("dp")
    nz = lax.axis_size("tensor")
    tok, width = section_input.shape[1:]
    feat = weights.shape[1]
    cols = weights.shape[2]
    assert nd == nz and feat == cols
    sub = tok // nz
    piece = R * R // nz
    queries = query_grads.shape[1]
    column = sections * nz
    plane = nd * nz
    vmem = pl.BlockSpec(memory_space=pltpu.VMEM)
    hbm = pl.BlockSpec(memory_space=pl.ANY)
    dma = pltpu.SemaphoreType.DMA
    sems = []
    for count in (nd, nd, nz, nd, nz, nd, plane):
        sems += [dma((count,)), dma((count,))]
    sems += [dma((nz,)), dma((nd,)), dma((1,)), dma((1,))]
    sems += [dma((plane,)), dma((plane,)), dma((column,)), dma((column,))]
    grads, scores = pl.pallas_call(
        functools.partial(kernel, sections, nd, nz),
        out_shape=(
            jax.ShapeDtypeStruct((SEQS, piece), F32),
            jax.ShapeDtypeStruct((SEQS, queries), F32),
        ),
        in_specs=[hbm, hbm, vmem, pl.BlockSpec(memory_space=pltpu.SMEM), hbm, vmem],
        out_specs=(vmem, vmem),
        scratch_shapes=[
            pltpu.VMEM((nd, tok, feat), BF16),
            pltpu.VMEM((nd, sub, R), F32),
            pltpu.VMEM((nz, nd, sub, cols), BF16),
            pltpu.VMEM((nz, nd, sub, cols), BF16),
            pltpu.VMEM((nd, sub, cols), F32),
            pltpu.VMEM((nd, sub, cols), BF16),
            pltpu.VMEM((tok, feat), BF16),
            pltpu.VMEM((nz, nd, sub, cols), BF16),
            pltpu.VMEM((nd, nz, sub, feat), BF16),
            pltpu.VMEM((nd, nz, sub, feat), BF16),
            pltpu.VMEM((plane, 8, tok), F32),
            pltpu.VMEM((tok, feat), BF16),
            pltpu.VMEM((nz, SEQS, piece), F32),
            pltpu.VMEM((plane, SEQS, piece), F32),
            pltpu.VMEM((column, SEQS, queries), F32),
            pltpu.VMEM((tok, width), BF16),
            pltpu.VMEM((feat, cols), BF16),
            pltpu.VMEM((nd, sub, cols), F32),
            pltpu.VMEM((tok, feat), F32),
            pltpu.VMEM((tok, 128), F32),
            pltpu.VMEM((tok, tok), F32),
            pltpu.VMEM((nz, sub, tok), F32),
            *sems,
            dma((4,)),
            pltpu.SemaphoreType.REGULAR((2,)),
        ],
        compiler_params=pltpu.CompilerParams(
            collective_id=0, has_side_effects=True, vmem_limit_bytes=60 * 1024 * 1024
        ),
    )(section_input[0], weights[0], gains, proj_seeds, out_grad, query_grads[0])
    return (grads[None], scores)


def solution(mesh):
    in_specs = (
        P("section", "dp", None),
        P("section", "tensor", "dp"),
        P("section", None),
        P("section", None),
        P("dp", None),
        P("section", "dp", "tensor"),
    )
    out_specs = (P("section", None, "tensor"), P(None, "dp"))
    return jax.shard_map(body, mesh=mesh, in_specs=in_specs, out_specs=out_specs, check_vma=False)
```

```python
import functools
import math

import jax
import jax.numpy as jnp
from jax import lax
from jax.experimental import pallas as pl
from jax.experimental.pallas import tpu as pltpu
from jax.sharding import PartitionSpec as P

R = 64
SEQS = 2
eps = 1e-05
F32 = jnp.float32
BF16 = jnp.bfloat16
MESH = pl.DeviceIdType.MESH
NT = (((1,), (1,)), ((), ()))


def sign_rows(seed_value, row_start, row_count, scale):
    row_index = lax.broadcasted_iota(jnp.int32, (R, row_count), 1) + row_start
    col_index = lax.broadcasted_iota(jnp.int32, (R, row_count), 0)
    mixing = row_index * 40503 + col_index * 9973 + (seed_value * 7919 + 12345)
    mixing = mixing ^ (mixing >> 13)
    mixing = mixing * 1274126177
    mixing = mixing ^ (mixing >> 16)
    parity = (mixing >> 10) & 1
    return jnp.where(parity == 1, scale, -scale).astype(BF16)


def kernel(
    sections, nd, nz,
    x_hbm, w_hbm, gain_ref, seed_ref, og_ref, q_ref,
    grads_ref, scores_ref,
    a_buf, inf_buf, ps_buf, pr_buf, slope_buf, ui_buf, uii_buf, gp_buf,
    gns_buf, gnr_buf, dot_buf, up_buf, g_buf, gr_buf, sc_buf,
    x_ref, w_ref, sum_buf, norm_buf, rad_buf, turn_buf, mean_buf,
    a_ss, a_rs, inf_ss, inf_rs, p_ss, p_rs, og_ss, og_rs, gp_ss, gp_rs,
    gn_ss, gn_rs, dt_ss, dt_rs, up_ss, up_rs, uii_ss, uii_rs,
    g_ss, g_rs, sc_ss, sc_rs, in_sem, go_sem,
):
    s = lax.axis_index("section")
    d = lax.axis_index("dp")
    z = lax.axis_index("tensor")
    tok, width = x_hbm.shape
    feat = width // nz
    cols = width // nd
    sub = tok // nz
    at_top = s == sections - 1
    below_top = s == sections - 2
    lower = s > 0
    z_start = pl.multiple_of(z * feat, feat)
    d_start = pl.multiple_of(d * cols, cols)
    sub_start = pl.multiple_of(z * sub, sub)
    sub_start_d = pl.multiple_of(d * sub, sub)

    def dev(s_to, d_to, z_to):
        return {"section": s_to, "dp": d_to, "tensor": z_to}

    def remote(src, dst, ss, rs, to):
        return pltpu.make_async_remote_copy(
            src_ref=src, dst_ref=dst, send_sem=ss, recv_sem=rs, device_id=to, device_id_type=MESH
        )

    x_load = pltpu.make_async_copy(x_hbm, x_ref, in_sem.at[0])
    w_load = pltpu.make_async_copy(w_hbm, w_ref, in_sem.at[1])
    x_load.start()
    w_load.start()

    barrier = pltpu.get_barrier_semaphore()
    total = sections * nd * nz
    me = (s * nd + d) * nz + z

    @pl.loop(1, total)
    def _(step):
        other = lax.rem(me + step, total)
        pl.semaphore_signal(
            barrier, inc=1, device_id_type=MESH,
            device_id=dev(other // (nd * nz), lax.rem(other // nz, nd), lax.rem(other, nz)),
        )

    x_load.wait()
    hidden = x_ref[...].astype(F32)
    radius = jnp.sqrt(jnp.mean(hidden * hidden, axis=1, keepdims=True) + eps)
    gain_z = gain_ref[:, pl.ds(z_start, feat)]
    normed_z = x_ref[:, pl.ds(z_start, feat)].astype(F32) / radius
    norm_buf[...] = normed_z
    rad_buf[...] = jnp.broadcast_to(radius, rad_buf.shape)
    a_buf[d] = (normed_z * gain_z).astype(BF16)

    pl.semaphore_wait(barrier, total - 1)

    def a_copy(o):
        to = lax.rem(d + o, nd)
        return remote(a_buf.at[d], a_buf.at[d], a_ss.at[o], a_rs.at[o], dev(s, to, z))

    @pl.when(jnp.logical_not(below_top))
    def _():
        for o in range(1, nd):
            a_copy(o).start()

    def og_copy(o):
        to = lax.rem(d + o, nd)
        src = og_ref.at[pl.ds(sub_start, sub), pl.ds(pl.multiple_of(to * cols, cols), cols)]
        return remote(src, ui_buf.at[d], og_ss.at[o], og_rs.at[o], dev(s, to, z))

    def ui_load():
        src = og_ref.at[pl.ds(sub_start, sub), pl.ds(d_start, cols)]
        return pltpu.make_async_copy(src, ui_buf.at[d], in_sem.at[2])

    def uii_load():
        return pltpu.make_async_copy(og_ref.at[:, pl.ds(z_start, feat)], uii_buf, in_sem.at[3])

    @pl.when(at_top)
    def _():
        for o in range(1, nd):
            og_copy(o).start()
        ui_load().start()
        uii_load().start()

    scale = 1.0 / math.sqrt(width)
    x_sub = x_ref[pl.ds(sub_start, sub), :].astype(F32)
    radius_sub = jnp.sqrt(jnp.mean(x_sub * x_sub, axis=1, keepdims=True) + eps)
    lifted_sub = (x_sub / radius_sub * gain_ref[...]).astype(BF16)
    table_in = sign_rows(seed_ref[0, 0], 0, width, scale)
    inf_buf[d] = lax.dot_general(lifted_sub, table_in, NT, preferred_element_type=F32)

    def inf_copy(o):
        to = lax.rem(d + o, nd)
        return remote(inf_buf.at[d], inf_buf.at[d], inf_ss.at[o], inf_rs.at[o], dev(s, to, z))

    for o in range(1, nd):
        inf_copy(o).start()

    @pl.when(below_top)
    def _():
        pl.semaphore_wait(go_sem.at[0], 1)
        for o in range(1, nd):
            a_copy(o).start()

    w_load.wait()

    def p_copy(o, block):
        to = lax.rem(z + o, nz)
        return remote(
            ps_buf.at[to, block], pr_buf.at[z, block], p_ss.at[o, block], p_rs.at[o, block],
            dev(s, d, to),
        )

    for o in range(nd):
        block = lax.rem(d + nd - o, nd)
        if o:
            a_copy(o).wait_recv()
        part = jnp.dot(a_buf[block], w_ref[...], preferred_element_type=F32).astype(BF16)
        for zt in range(nz):
            ps_buf[zt, block] = part[zt * sub : (zt + 1) * sub, :]

        @pl.when(jnp.logical_not(below_top))
        def _():
            for oz in range(1, nz):
                p_copy(oz, block).start()

    for o in range(1, nd):
        a_copy(o).wait_send()

    def go(which):
        pl.semaphore_signal(
            go_sem.at[which], inc=1, device_id=dev(jnp.maximum(s - 1, 0), d, z), device_id_type=MESH
        )

    if sections > 1:
        @pl.when(at_top)
        def _():
            go(0)

        @pl.when(below_top)
        def _():
            pl.semaphore_wait(go_sem.at[1], 1)
            for o in range(nd):
                block = lax.rem(d + nd - o, nd)
                for oz in range(1, nz):
                    p_copy(oz, block).start()

    table_out = sign_rows(seed_ref[0, 1], d_start, cols, scale)

    def gp_copy(o, block):
        to = lax.rem(z + o, nz)
        return remote(
            gp_buf.at[z, block], gp_buf.at[z, block], gp_ss.at[o, block], gp_rs.at[o, block],
            dev(s, d, to),
        )

    for o in range(nd):
        block = lax.rem(d + nd - o, nd)
        summed = ps_buf[z, block].astype(F32)
        for oz in range(1, nz):
            p_copy(oz, block).wait_recv()
            summed = summed + pr_buf[lax.rem(z + nz - oz, nz), block].astype(F32)
        sig = jax.nn.sigmoid(summed)
        slope = sig * (1.0 + summed * (1.0 - sig))
        sum_buf[block] = summed
        slope_buf[block] = slope

        @pl.when(at_top)
        def _():
            if o:
                og_copy(o).wait_recv()
            else:
                ui_load().wait()
            gp_buf[z, block] = (ui_buf[block].astype(F32) * slope).astype(BF16)
            if sections > 1:
                for oz in range(1, nz):
                    gp_copy(oz, block).start()

    def up_copy(zt, source):
        return remote(
            up_buf.at[pl.ds(zt * sub, sub)], ui_buf.at[source], up_ss.at[zt], up_rs.at[source],
            dev(jnp.maximum(s - 1, 0), z, zt),
        )

    def uii_copy():
        return remote(up_buf, uii_buf, uii_ss.at[0], uii_rs.at[0], dev(jnp.maximum(s - 1, 0), d, z))

    @pl.when(at_top)
    def _():
        uii_load().wait()

    @pl.when(jnp.logical_not(at_top))
    def _():
        for source in range(nd):
            up_copy(0, source).wait_recv()
        gp_buf[z] = (ui_buf[...].astype(F32) * slope_buf[...]).astype(BF16)

        @pl.when(lower)
        def _():
            for block in range(nd):
                for oz in range(1, nz):
                    gp_copy(oz, block).start()

    grad_pre = gp_buf[z]
    plane = nd * nz
    mine = d * nz + z

    def dt_copy(o):
        to = lax.rem(mine + o, plane)
        return remote(
            dot_buf.at[mine], dot_buf.at[mine], dt_ss.at[o], dt_rs.at[o],
            dev(s, to // nz, lax.rem(to, nz)),
        )

    @pl.when(lower)
    def _():
        pre = gp_buf[z].astype(F32) * sum_buf[...]
        own_dot = jnp.sum(pre.reshape(nd * sub, cols), axis=1, keepdims=True)
        dot_buf[mine] = jnp.broadcast_to(own_dot, (tok, tok)).T[:8, :]
        for o in range(1, plane):
            dt_copy(o).start()

    for o in range(1, nd):
        inf_copy(o).wait_recv()
    out_feat = lax.dot_general(
        grad_pre.reshape(nd * sub, cols), table_out, NT, preferred_element_type=F32
    ).astype(BF16)
    in_feat = inf_buf[...].reshape(nd * sub, R).astype(BF16)
    piece = R * R // nz
    per_seq = nd * sub // SEQS
    for zt in range(nz):
        entry = lax.broadcasted_iota(jnp.int32, (R, piece), 1) + zt * piece
        which = lax.broadcasted_iota(jnp.int32, (R, piece), 0)
        pick_in = (entry // R == which).astype(F32).astype(BF16)
        pick_out = (entry % R == which).astype(F32).astype(BF16)
        left = jnp.dot(in_feat, pick_in, preferred_element_type=F32)
        right = jnp.dot(out_feat, pick_out, preferred_element_type=F32)
        product = left * right
        for k in range(SEQS):
            g_buf[zt, k : k + 1, :] = jnp.sum(
                product[k * per_seq : (k + 1) * per_seq], axis=0, keepdims=True
            )

    def g_copy(o):
        to = lax.rem(mine + o, plane)
        return remote(
            g_buf.at[lax.rem(to, nz)], gr_buf.at[mine], g_ss.at[o], g_rs.at[o],
            dev(s, to // nz, lax.rem(to, nz)),
        )

    for o in range(1, plane):
        g_copy(o).start()
    gr_buf[mine] = g_buf[z]

    def gn_copy(o):
        to = lax.rem(d + nd - o, nd)
        return remote(gns_buf.at[to], gnr_buf.at[d], gn_ss.at[o], gn_rs.at[o], dev(s, to, z))

    @pl.when(lower)
    def _():
        for o in range(nd):
            block = lax.rem(d + nd - o, nd)
            for oz in range(1, nz):
                gp_copy(oz, block).wait_recv()
            rows = gp_buf[:, block].reshape(tok, cols)
            part = lax.dot_general(rows, w_ref[...], NT, preferred_element_type=F32).astype(BF16)
            if o:
                gns_buf[block] = part
                gn_copy(o).start()
            else:
                gnr_buf[d] = part
        for block in range(nd):
            for oz in range(1, nz):
                gp_copy(oz, block).wait_send()

        @pl.when(at_top)
        def _():
            go(1)

        for o in range(1, plane):
            dt_copy(o).wait_recv()
        for zt in range(nz):
            dots = dot_buf[zt]
            for dt in range(1, nd):
                dots = dots + dot_buf[dt * nz + zt]
            turn_buf[...] = jnp.broadcast_to(dots[:1, :] * (1.0 / width), (tok, tok)).T
            mean_buf[zt] = turn_buf[pl.ds(sub_start_d, sub), :]
        for o in range(1, nd):
            gn_copy(o).wait_recv()
        grad_norm = gnr_buf[0].astype(F32)
        for dt in range(1, nd):
            grad_norm = grad_norm + gnr_buf[dt].astype(F32)
        grad_norm = grad_norm.astype(BF16).astype(F32)
        scaled = grad_norm * gain_ref[:, pl.ds(z_start, feat)]
        normed = norm_buf[...]
        rad = rad_buf[:, :1]
        mean_dot = mean_buf[...].reshape(tok, tok)[:, :1]
        if sections > 2:
            @pl.when(jnp.logical_not(at_top))
            def _():
                uii_copy().wait_recv()
        up_buf[...] = (uii_buf[...].astype(F32) + (scaled - normed * mean_dot) / rad).astype(BF16)
        for zt in range(nz):
            up_copy(zt, d).start()
        if sections > 2:
            @pl.when(s > 1)
            def _():
                uii_copy().start()

    for o in range(1, plane):
        g_copy(o).wait_recv()
    grads = gr_buf[0]
    for other in range(1, plane):
        grads = grads + gr_buf[other]
    grads_ref[...] = grads
    queries = q_ref[...]
    high = grads.astype(BF16)
    rest = grads - high.astype(F32)
    middle = rest.astype(BF16)
    low = (rest - middle.astype(F32)).astype(BF16)
    part = lax.dot_general(high, queries, NT, preferred_element_type=F32)
    part = part + lax.dot_general(middle, queries, NT, preferred_element_type=F32)
    part = part + lax.dot_general(low, queries, NT, preferred_element_type=F32)
    column = sections * nz
    here = s * nz + z
    sc_buf[here] = part

    def sc_copy(o):
        to = lax.rem(here + o, column)
        return remote(
            sc_buf.at[here], sc_buf.at[here], sc_ss.at[o], sc_rs.at[o],
            dev(to // nz, d, lax.rem(to, nz)),
        )

    for o in range(1, column):
        sc_copy(o).start()

    for o in range(1, nd):
        inf_copy(o).wait_send()
    for block in range(nd):
        for oz in range(1, nz):
            p_copy(oz, block).wait_send()

    @pl.when(at_top)
    def _():
        for o in range(1, nd):
            og_copy(o).wait_send()

    @pl.when(lower)
    def _():
        for o in range(1, plane):
            dt_copy(o).wait_send()
        for o in range(1, nd):
            gn_copy(o).wait_send()
        for zt in range(nz):
            up_copy(zt, d).wait_send()
        if sections > 2:
            @pl.when(s > 1)
            def _():
                uii_copy().wait_send()

    for o in range(1, plane):
        g_copy(o).wait_send()
    for o in range(1, column):
        sc_copy(o).wait_recv()
    scores = sc_buf[0]
    for other in range(1, column):
        scores = scores + sc_buf[other]
    scores_ref[...] = scores
    for o in range(1, column):
        sc_copy(o).wait_send()


def body(section_input, weights, gains, proj_seeds, out_grad, query_grads):
    sections = lax.axis_size("section")
    nd = lax.axis_size("dp")
    nz = lax.axis_size("tensor")
    tok, width = section_input.shape[1:]
    feat = weights.shape[1]
    cols = weights.shape[2]
    assert nd == nz and feat == cols
    sub = tok // nz
    piece = R * R // nz
    queries = query_grads.shape[1]
    column = sections * nz
    plane = nd * nz
    vmem = pl.BlockSpec(memory_space=pltpu.VMEM)
    hbm = pl.BlockSpec(memory_space=pl.ANY)
    dma = pltpu.SemaphoreType.DMA
    sems = []
    for shape in ((nd,), (nd,), (nz, nd), (nd,), (nz, nd), (nd,), (plane,)):
        sems += [dma(shape), dma(shape)]
    sems += [dma((nz,)), dma((nd,)), dma((1,)), dma((1,))]
    sems += [dma((plane,)), dma((plane,)), dma((column,)), dma((column,))]
    grads, scores = pl.pallas_call(
        functools.partial(kernel, sections, nd, nz),
        out_shape=(
            jax.ShapeDtypeStruct((SEQS, piece), F32),
            jax.ShapeDtypeStruct((SEQS, queries), F32),
        ),
        in_specs=[hbm, hbm, vmem, pl.BlockSpec(memory_space=pltpu.SMEM), hbm, vmem],
        out_specs=(vmem, vmem),
        scratch_shapes=[
            pltpu.VMEM((nd, tok, feat), BF16),
            pltpu.VMEM((nd, sub, R), F32),
            pltpu.VMEM((nz, nd, sub, cols), BF16),
            pltpu.VMEM((nz, nd, sub, cols), BF16),
            pltpu.VMEM((nd, sub, cols), F32),
            pltpu.VMEM((nd, sub, cols), BF16),
            pltpu.VMEM((tok, feat), BF16),
            pltpu.VMEM((nz, nd, sub, cols), BF16),
            pltpu.VMEM((nd, tok, feat), BF16),
            pltpu.VMEM((nd, tok, feat), BF16),
            pltpu.VMEM((plane, 8, tok), F32),
            pltpu.VMEM((tok, feat), BF16),
            pltpu.VMEM((nz, SEQS, piece), F32),
            pltpu.VMEM((plane, SEQS, piece), F32),
            pltpu.VMEM((column, SEQS, queries), F32),
            pltpu.VMEM((tok, width), BF16),
            pltpu.VMEM((feat, cols), BF16),
            pltpu.VMEM((nd, sub, cols), F32),
            pltpu.VMEM((tok, feat), F32),
            pltpu.VMEM((tok, 128), F32),
            pltpu.VMEM((tok, tok), F32),
            pltpu.VMEM((nz, sub, tok), F32),
            *sems,
            dma((4,)),
            pltpu.SemaphoreType.REGULAR((2,)),
        ],
        compiler_params=pltpu.CompilerParams(
            collective_id=0, has_side_effects=True, vmem_limit_bytes=60 * 1024 * 1024
        ),
    )(section_input[0], weights[0], gains, proj_seeds, out_grad, query_grads[0])
    return (grads[None], scores)


def solution(mesh):
    in_specs = (
        P("section", "dp", None),
        P("section", "tensor", "dp"),
        P("section", None),
        P("section", None),
        P("dp", None),
        P("section", "dp", "tensor"),
    )
    out_specs = (P("section", None, "tensor"), P(None, "dp"))
    return jax.shard_map(body, mesh=mesh, in_specs=in_specs, out_specs=out_specs, check_vma=False)
```

```python
import functools
import math

import jax
import jax.numpy as jnp
from jax import lax
from jax.experimental import pallas as pl
from jax.experimental.pallas import tpu as pltpu
from jax.sharding import PartitionSpec as P

R = 64
SEQS = 2
eps = 1e-05
F32 = jnp.float32
BF16 = jnp.bfloat16
MESH = pl.DeviceIdType.MESH
NT = (((1,), (1,)), ((), ()))


def sign_rows(seed_value, row_start, row_count, scale):
    row_index = lax.broadcasted_iota(jnp.int32, (R, row_count), 1) + row_start
    col_index = lax.broadcasted_iota(jnp.int32, (R, row_count), 0)
    mixing = row_index * 40503 + col_index * 9973 + (seed_value * 7919 + 12345)
    mixing = mixing ^ (mixing >> 13)
    mixing = mixing * 1274126177
    mixing = mixing ^ (mixing >> 16)
    parity = (mixing >> 10) & 1
    return jnp.where(parity == 1, scale, -scale).astype(BF16)


def kernel(
    sections, nd, nz,
    x_hbm, w_hbm, gain_ref, seed_ref, og_ref, q_ref,
    out_ref,
    a_buf, inf_buf, ps_buf, pr_buf, slope_buf, ui_buf, uii_buf, gp_buf,
    gns_buf, gnr_buf, dot_buf, up_buf, g_buf, gr_buf, sc_buf,
    x_ref, w_ref, sum_buf, norm_buf, rad_buf, turn_buf, mean_buf, left_buf, pick_buf,
    a_ss, a_rs, inf_ss, inf_rs, p_ss, p_rs, og_ss, og_rs, gp_ss, gp_rs,
    gn_ss, gn_rs, dt_ss, dt_rs, up_ss, up_rs, uii_ss, uii_rs,
    g_ss, g_rs, sc_ss, sc_rs, in_sem, go_sem,
):
    s = lax.axis_index("section")
    d = lax.axis_index("dp")
    z = lax.axis_index("tensor")
    tok, width = x_hbm.shape
    feat = width // nz
    cols = width // nd
    sub = tok // nz
    at_top = s == sections - 1
    below_top = s == sections - 2
    lower = s > 0
    z_start = pl.multiple_of(z * feat, feat)
    d_start = pl.multiple_of(d * cols, cols)
    sub_start = pl.multiple_of(z * sub, sub)
    sub_start_d = pl.multiple_of(d * sub, sub)

    def dev(s_to, d_to, z_to):
        return {"section": s_to, "dp": d_to, "tensor": z_to}

    def remote(src, dst, ss, rs, to):
        return pltpu.make_async_remote_copy(
            src_ref=src, dst_ref=dst, send_sem=ss, recv_sem=rs, device_id=to, device_id_type=MESH
        )

    x_load = pltpu.make_async_copy(x_hbm, x_ref, in_sem.at[0])
    w_load = pltpu.make_async_copy(w_hbm, w_ref, in_sem.at[1])
    x_load.start()
    w_load.start()

    barrier = pltpu.get_barrier_semaphore()
    total = sections * nd * nz
    me = (s * nd + d) * nz + z

    @pl.loop(1, total)
    def _(step):
        other = lax.rem(me + step, total)
        pl.semaphore_signal(
            barrier, inc=1, device_id_type=MESH,
            device_id=dev(other // (nd * nz), lax.rem(other // nz, nd), lax.rem(other, nz)),
        )

    x_load.wait()
    hidden = x_ref[...].astype(F32)
    radius = jnp.sqrt(jnp.mean(hidden * hidden, axis=1, keepdims=True) + eps)
    gain_z = gain_ref[:, pl.ds(z_start, feat)]
    normed_z = x_ref[:, pl.ds(z_start, feat)].astype(F32) / radius
    norm_buf[...] = normed_z
    rad_buf[...] = jnp.broadcast_to(radius, rad_buf.shape)
    a_buf[d] = (normed_z * gain_z).astype(BF16)

    pl.semaphore_wait(barrier, total - 1)

    def a_copy(o):
        to = lax.rem(d + o, nd)
        return remote(a_buf.at[d], a_buf.at[d], a_ss.at[o], a_rs.at[o], dev(s, to, z))

    @pl.when(jnp.logical_not(below_top))
    def _():
        for o in range(1, nd):
            a_copy(o).start()

    def og_copy(o):
        to = lax.rem(d + o, nd)
        src = og_ref.at[pl.ds(sub_start, sub), pl.ds(pl.multiple_of(to * cols, cols), cols)]
        return remote(src, ui_buf.at[d], og_ss.at[o], og_rs.at[o], dev(s, to, z))

    def ui_load():
        src = og_ref.at[pl.ds(sub_start, sub), pl.ds(d_start, cols)]
        return pltpu.make_async_copy(src, ui_buf.at[d], in_sem.at[2])

    def uii_load():
        return pltpu.make_async_copy(og_ref.at[:, pl.ds(z_start, feat)], uii_buf, in_sem.at[3])

    @pl.when(at_top)
    def _():
        for o in range(1, nd):
            og_copy(o).start()
        ui_load().start()
        uii_load().start()

    @pl.when(below_top)
    def _():
        pl.semaphore_wait(go_sem.at[0], 1)
        for o in range(1, nd):
            a_copy(o).start()

    w_load.wait()

    def p_copy(o, block):
        to = lax.rem(z + o, nz)
        return remote(
            ps_buf.at[to, block], pr_buf.at[z, block], p_ss.at[o, block], p_rs.at[o, block],
            dev(s, d, to),
        )

    for o in range(nd):
        block = lax.rem(d + nd - o, nd)
        if o:
            a_copy(o).wait_recv()
        part = jnp.dot(a_buf[block], w_ref[...], preferred_element_type=F32).astype(BF16)
        for zt in range(nz):
            ps_buf[zt, block] = part[zt * sub : (zt + 1) * sub, :]

        @pl.when(jnp.logical_not(below_top))
        def _():
            for oz in range(1, nz):
                p_copy(oz, block).start()

    for o in range(1, nd):
        a_copy(o).wait_send()

    def go(which):
        pl.semaphore_signal(
            go_sem.at[which], inc=1, device_id=dev(jnp.maximum(s - 1, 0), d, z), device_id_type=MESH
        )

    if sections > 1:
        @pl.when(at_top)
        def _():
            go(0)

    scale = 1.0 / math.sqrt(width)
    x_sub = x_ref[pl.ds(sub_start, sub), :].astype(F32)
    radius_sub = jnp.sqrt(jnp.mean(x_sub * x_sub, axis=1, keepdims=True) + eps)
    lifted_sub = (x_sub / radius_sub * gain_ref[...]).astype(BF16)
    table_in = sign_rows(seed_ref[0, 0], 0, width, scale)
    inf_buf[d] = lax.dot_general(lifted_sub, table_in, NT, preferred_element_type=F32)

    def inf_copy(o):
        to = lax.rem(d + o, nd)
        return remote(inf_buf.at[d], inf_buf.at[d], inf_ss.at[o], inf_rs.at[o], dev(s, to, z))

    for o in range(1, nd):
        inf_copy(o).start()


    piece = R * R // nz
    per_seq = nd * sub // SEQS

    def spread():
        for o in range(1, nd):
            inf_copy(o).wait_recv()
        in_feat = inf_buf[...].reshape(nd * sub, R).astype(BF16)
        for zt in range(nz):
            entry = lax.broadcasted_iota(jnp.int32, (R, piece), 1) + zt * piece
            which = lax.broadcasted_iota(jnp.int32, (R, piece), 0)
            pick_in = (entry // R == which).astype(F32).astype(BF16)
            pick_buf[zt] = (entry % R == which).astype(F32).astype(BF16)
            left_buf[zt] = jnp.dot(in_feat, pick_in, preferred_element_type=F32)

    @pl.when(jnp.logical_not(at_top))
    def _():
        spread()

    if sections > 1:
        @pl.when(below_top)
        def _():
            pl.semaphore_wait(go_sem.at[1], 1)
            for o in range(nd):
                block = lax.rem(d + nd - o, nd)
                for oz in range(1, nz):
                    p_copy(oz, block).start()

    table_out = sign_rows(seed_ref[0, 1], d_start, cols, scale)

    def gp_copy(o, block):
        to = lax.rem(z + o, nz)
        return remote(
            gp_buf.at[z, block], gp_buf.at[z, block], gp_ss.at[o, block], gp_rs.at[o, block],
            dev(s, d, to),
        )

    for o in range(nd):
        block = lax.rem(d + nd - o, nd)
        summed = ps_buf[z, block].astype(F32)
        for oz in range(1, nz):
            p_copy(oz, block).wait_recv()
            summed = summed + pr_buf[lax.rem(z + nz - oz, nz), block].astype(F32)
        sig = jax.nn.sigmoid(summed)
        slope = sig * (1.0 + summed * (1.0 - sig))
        sum_buf[block] = summed
        slope_buf[block] = slope

        @pl.when(at_top)
        def _():
            if o:
                og_copy(o).wait_recv()
            else:
                ui_load().wait()
            gp_buf[z, block] = (ui_buf[block].astype(F32) * slope).astype(BF16)
            if sections > 1:
                for oz in range(1, nz):
                    gp_copy(oz, block).start()

    def up_copy(zt, source):
        return remote(
            up_buf.at[pl.ds(zt * sub, sub)], ui_buf.at[source], up_ss.at[zt], up_rs.at[source],
            dev(jnp.maximum(s - 1, 0), z, zt),
        )

    def uii_copy():
        return remote(up_buf, uii_buf, uii_ss.at[0], uii_rs.at[0], dev(jnp.maximum(s - 1, 0), d, z))

    @pl.when(at_top)
    def _():
        uii_load().wait()
        spread()

    @pl.when(jnp.logical_not(at_top))
    def _():
        for source in range(nd):
            up_copy(0, source).wait_recv()
        gp_buf[z] = (ui_buf[...].astype(F32) * slope_buf[...]).astype(BF16)

        @pl.when(lower)
        def _():
            for block in range(nd):
                for oz in range(1, nz):
                    gp_copy(oz, block).start()

    grad_pre = gp_buf[z]
    plane = nd * nz
    mine = d * nz + z

    def dt_copy(o):
        to = lax.rem(mine + o, plane)
        return remote(
            dot_buf.at[mine], dot_buf.at[mine], dt_ss.at[o], dt_rs.at[o],
            dev(s, to // nz, lax.rem(to, nz)),
        )

    @pl.when(lower)
    def _():
        pre = gp_buf[z].astype(F32) * sum_buf[...]
        own_dot = jnp.sum(pre.reshape(nd * sub, cols), axis=1, keepdims=True)
        dot_buf[mine] = jnp.broadcast_to(own_dot, (tok, tok)).T[:8, :]
        for o in range(1, plane):
            dt_copy(o).start()

    out_feat = lax.dot_general(
        grad_pre.reshape(nd * sub, cols), table_out, NT, preferred_element_type=F32
    ).astype(BF16)
    for zt in range(nz):
        product = left_buf[zt] * jnp.dot(out_feat, pick_buf[zt], preferred_element_type=F32)
        for k in range(SEQS):
            g_buf[zt, k : k + 1, :] = jnp.sum(
                product[k * per_seq : (k + 1) * per_seq], axis=0, keepdims=True
            )

    def g_copy(o):
        to = lax.rem(mine + o, plane)
        return remote(
            g_buf.at[lax.rem(to, nz)], gr_buf.at[mine], g_ss.at[o], g_rs.at[o],
            dev(s, to // nz, lax.rem(to, nz)),
        )

    for o in range(1, plane):
        g_copy(o).start()
    gr_buf[mine] = g_buf[z]

    def gn_copy(o):
        to = lax.rem(d + nd - o, nd)
        return remote(gns_buf.at[to], gnr_buf.at[d], gn_ss.at[o], gn_rs.at[o], dev(s, to, z))

    @pl.when(lower)
    def _():
        for o in range(nd):
            block = lax.rem(d + nd - o, nd)
            for oz in range(1, nz):
                gp_copy(oz, block).wait_recv()
            if o == nd - 1:
                for each in range(nd):
                    for oz in range(1, nz):
                        gp_copy(oz, each).wait_send()

                @pl.when(at_top)
                def _():
                    go(1)

            rows = gp_buf[:, block].reshape(tok, cols)
            part = lax.dot_general(rows, w_ref[...], NT, preferred_element_type=F32).astype(BF16)
            if o:
                gns_buf[block] = part
                gn_copy(o).start()
            else:
                gnr_buf[d] = part
        for o in range(1, plane):
            dt_copy(o).wait_recv()
        for zt in range(nz):
            dots = dot_buf[zt]
            for dt in range(1, nd):
                dots = dots + dot_buf[dt * nz + zt]
            turn_buf[...] = jnp.broadcast_to(dots[:1, :] * (1.0 / width), (tok, tok)).T
            mean_buf[zt] = turn_buf[pl.ds(sub_start_d, sub), :]
        for o in range(1, nd):
            gn_copy(o).wait_recv()
        grad_norm = gnr_buf[0].astype(F32)
        for dt in range(1, nd):
            grad_norm = grad_norm + gnr_buf[dt].astype(F32)
        grad_norm = grad_norm.astype(BF16).astype(F32)
        scaled = grad_norm * gain_ref[:, pl.ds(z_start, feat)]
        normed = norm_buf[...]
        rad = rad_buf[:, :1]
        mean_dot = mean_buf[...].reshape(tok, tok)[:, :1]
        if sections > 2:
            @pl.when(jnp.logical_not(at_top))
            def _():
                uii_copy().wait_recv()
        up_buf[...] = (uii_buf[...].astype(F32) + (scaled - normed * mean_dot) / rad).astype(BF16)
        for zt in range(nz):
            up_copy(zt, d).start()
        if sections > 2:
            @pl.when(s > 1)
            def _():
                uii_copy().start()

    for o in range(1, plane):
        g_copy(o).wait_recv()
    grads = gr_buf[0]
    for other in range(1, plane):
        grads = grads + gr_buf[other]
    out_ref[:, :piece] = grads
    queries = q_ref[...]
    high = grads.astype(BF16)
    rest = grads - high.astype(F32)
    middle = rest.astype(BF16)
    low = (rest - middle.astype(F32)).astype(BF16)
    part = lax.dot_general(high, queries, NT, preferred_element_type=F32)
    part = part + lax.dot_general(middle, queries, NT, preferred_element_type=F32)
    part = part + lax.dot_general(low, queries, NT, preferred_element_type=F32)
    column = sections * nz
    here = s * nz + z
    sc_buf[here] = part

    def sc_copy(o):
        to = lax.rem(here + o, column)
        return remote(
            sc_buf.at[here], sc_buf.at[here], sc_ss.at[o], sc_rs.at[o],
            dev(to // nz, d, lax.rem(to, nz)),
        )

    for o in range(1, column):
        sc_copy(o).start()

    for o in range(1, nd):
        inf_copy(o).wait_send()
    for block in range(nd):
        for oz in range(1, nz):
            p_copy(oz, block).wait_send()

    @pl.when(at_top)
    def _():
        for o in range(1, nd):
            og_copy(o).wait_send()

    @pl.when(lower)
    def _():
        for o in range(1, plane):
            dt_copy(o).wait_send()
        for o in range(1, nd):
            gn_copy(o).wait_send()
        for zt in range(nz):
            up_copy(zt, d).wait_send()
        if sections > 2:
            @pl.when(s > 1)
            def _():
                uii_copy().wait_send()

    for o in range(1, plane):
        g_copy(o).wait_send()
    for o in range(1, column):
        sc_copy(o).wait_recv()
    scores = sc_buf[0]
    for other in range(1, column):
        scores = scores + sc_buf[other]
    out_ref[:, piece : piece + scores.shape[1]] = scores
    for o in range(1, column):
        sc_copy(o).wait_send()


def body(section_input, weights, gains, proj_seeds, out_grad, query_grads):
    sections = lax.axis_size("section")
    nd = lax.axis_size("dp")
    nz = lax.axis_size("tensor")
    tok, width = section_input.shape[1:]
    feat = weights.shape[1]
    cols = weights.shape[2]
    assert nd == nz and feat == cols
    sub = tok // nz
    piece = R * R // nz
    queries = query_grads.shape[1]
    column = sections * nz
    plane = nd * nz
    vmem = pl.BlockSpec(memory_space=pltpu.VMEM)
    hbm = pl.BlockSpec(memory_space=pl.ANY)
    dma = pltpu.SemaphoreType.DMA
    sems = []
    for shape in ((nd,), (nd,), (nz, nd), (nd,), (nz, nd), (nd,), (plane,)):
        sems += [dma(shape), dma(shape)]
    sems += [dma((nz,)), dma((nd,)), dma((1,)), dma((1,))]
    sems += [dma((plane,)), dma((plane,)), dma((column,)), dma((column,))]
    out = pl.pallas_call(
        functools.partial(kernel, sections, nd, nz),
        out_shape=jax.ShapeDtypeStruct((SEQS, piece + queries), F32),
        in_specs=[hbm, hbm, vmem, pl.BlockSpec(memory_space=pltpu.SMEM), hbm, vmem],
        out_specs=vmem,
        scratch_shapes=[
            pltpu.VMEM((nd, tok, feat), BF16),
            pltpu.VMEM((nd, sub, R), F32),
            pltpu.VMEM((nz, nd, sub, cols), BF16),
            pltpu.VMEM((nz, nd, sub, cols), BF16),
            pltpu.VMEM((nd, sub, cols), F32),
            pltpu.VMEM((nd, sub, cols), BF16),
            pltpu.VMEM((tok, feat), BF16),
            pltpu.VMEM((nz, nd, sub, cols), BF16),
            pltpu.VMEM((nd, tok, feat), BF16),
            pltpu.VMEM((nd, tok, feat), BF16),
            pltpu.VMEM((plane, 8, tok), F32),
            pltpu.VMEM((tok, feat), BF16),
            pltpu.VMEM((nz, SEQS, piece), F32),
            pltpu.VMEM((plane, SEQS, piece), F32),
            pltpu.VMEM((column, SEQS, queries), F32),
            pltpu.VMEM((tok, width), BF16),
            pltpu.VMEM((feat, cols), BF16),
            pltpu.VMEM((nd, sub, cols), F32),
            pltpu.VMEM((tok, feat), F32),
            pltpu.VMEM((tok, 128), F32),
            pltpu.VMEM((tok, tok), F32),
            pltpu.VMEM((nz, sub, tok), F32),
            pltpu.VMEM((nz, tok, piece), F32),
            pltpu.VMEM((nz, R, piece), BF16),
            *sems,
            dma((4,)),
            pltpu.SemaphoreType.REGULAR((2,)),
        ],
        compiler_params=pltpu.CompilerParams(
            collective_id=0, has_side_effects=True, vmem_limit_bytes=60 * 1024 * 1024
        ),
    )(section_input[0], weights[0], gains, proj_seeds, out_grad, query_grads[0])
    return (out[None, :, :piece], out[:, piece:])


def solution(mesh):
    in_specs = (
        P("section", "dp", None),
        P("section", "tensor", "dp"),
        P("section", None),
        P("section", None),
        P("dp", None),
        P("section", "dp", "tensor"),
    )
    out_specs = (P("section", None, "tensor"), P(None, "dp"))
    return jax.shard_map(body, mesh=mesh, in_specs=in_specs, out_specs=out_specs, check_vma=False)
```

```python
import functools
import math

import jax
import jax.numpy as jnp
from jax import lax
from jax.experimental import pallas as pl
from jax.experimental.pallas import tpu as pltpu
from jax.sharding import PartitionSpec as P

R = 64
SEQS = 2
eps = 1e-05
F32 = jnp.float32
BF16 = jnp.bfloat16
MESH = pl.DeviceIdType.MESH
NT = (((1,), (1,)), ((), ()))


def sign_rows(seed_value, row_start, row_count, scale):
    row_index = lax.broadcasted_iota(jnp.int32, (R, row_count), 1) + row_start
    col_index = lax.broadcasted_iota(jnp.int32, (R, row_count), 0)
    mixing = row_index * 40503 + col_index * 9973 + (seed_value * 7919 + 12345)
    mixing = mixing ^ (mixing >> 13)
    mixing = mixing * 1274126177
    mixing = mixing ^ (mixing >> 16)
    parity = (mixing >> 10) & 1
    return jnp.where(parity == 1, scale, -scale).astype(BF16)


def kernel(
    sections, nd, nz,
    x_hbm, w_hbm, gain_ref, seed_ref, og_ref, q_ref,
    out_ref,
    a_buf, inf_buf, ps_buf, pr_buf, slope_buf, ui_buf, uii_buf, gp_buf,
    gns_buf, gnr_buf, dot_buf, up_buf, g_buf, gr_buf, sc_buf,
    x_ref, w_ref, sum_buf, norm_buf, rad_buf, turn_buf, mean_buf, left_buf, pick_buf,
    a_ss, a_rs, inf_ss, inf_rs, p_ss, p_rs, og_ss, og_rs, gp_ss, gp_rs,
    gn_ss, gn_rs, dt_ss, dt_rs, up_ss, up_rs, uii_ss, uii_rs,
    g_ss, g_rs, sc_ss, sc_rs, in_sem, go_sem, far_sem,
):
    s = lax.axis_index("section")
    d = lax.axis_index("dp")
    z = lax.axis_index("tensor")
    tok, width = x_hbm.shape
    feat = width // nz
    cols = width // nd
    sub = tok // nz
    at_top = s == sections - 1
    below_top = s == sections - 2
    lower = s > 0
    z_start = pl.multiple_of(z * feat, feat)
    d_start = pl.multiple_of(d * cols, cols)
    sub_start = pl.multiple_of(z * sub, sub)
    sub_start_d = pl.multiple_of(d * sub, sub)

    def dev(s_to, d_to, z_to):
        return {"section": s_to, "dp": d_to, "tensor": z_to}

    def remote(src, dst, ss, rs, to):
        return pltpu.make_async_remote_copy(
            src_ref=src, dst_ref=dst, send_sem=ss, recv_sem=rs, device_id=to, device_id_type=MESH
        )

    x_load = pltpu.make_async_copy(x_hbm, x_ref, in_sem.at[0])
    w_load = pltpu.make_async_copy(w_hbm, w_ref, in_sem.at[1])
    x_load.start()
    w_load.start()

    barrier = pltpu.get_barrier_semaphore()
    column = sections * nz
    here = s * nz + z

    def signal_column(sem):
        for o in range(1, column):
            to = lax.rem(here + o, column)
            pl.semaphore_signal(
                sem, inc=1, device_id=dev(to // nz, d, lax.rem(to, nz)), device_id_type=MESH
            )

    for o in range(1, nd):
        pl.semaphore_signal(
            barrier, inc=1, device_id=dev(s, lax.rem(d + o, nd), z), device_id_type=MESH
        )
    signal_column(barrier)

    x_load.wait()
    hidden = x_ref[...].astype(F32)
    radius = jnp.sqrt(jnp.mean(hidden * hidden, axis=1, keepdims=True) + eps)
    gain_z = gain_ref[:, pl.ds(z_start, feat)]
    normed_z = x_ref[:, pl.ds(z_start, feat)].astype(F32) / radius
    norm_buf[...] = normed_z
    rad_buf[...] = jnp.broadcast_to(radius, rad_buf.shape)
    a_buf[d] = (normed_z * gain_z).astype(BF16)

    pl.semaphore_wait(barrier, nd - 1 + column - 1)

    def a_copy(o):
        to = lax.rem(d + o, nd)
        return remote(a_buf.at[d], a_buf.at[d], a_ss.at[o], a_rs.at[o], dev(s, to, z))

    @pl.when(jnp.logical_not(below_top))
    def _():
        for o in range(1, nd):
            a_copy(o).start()

    def og_copy(o):
        to = lax.rem(d + o, nd)
        src = og_ref.at[pl.ds(sub_start, sub), pl.ds(pl.multiple_of(to * cols, cols), cols)]
        return remote(src, ui_buf.at[d], og_ss.at[o], og_rs.at[o], dev(s, to, z))

    def ui_load():
        src = og_ref.at[pl.ds(sub_start, sub), pl.ds(d_start, cols)]
        return pltpu.make_async_copy(src, ui_buf.at[d], in_sem.at[2])

    def uii_load():
        return pltpu.make_async_copy(og_ref.at[:, pl.ds(z_start, feat)], uii_buf, in_sem.at[3])

    @pl.when(at_top)
    def _():
        for o in range(1, nd):
            og_copy(o).start()
        ui_load().start()
        uii_load().start()

    @pl.when(below_top)
    def _():
        pl.semaphore_wait(go_sem.at[0], 1)
        for o in range(1, nd):
            a_copy(o).start()

    signal_column(far_sem.at[0])

    w_load.wait()

    def p_copy(o, block):
        to = lax.rem(z + o, nz)
        return remote(
            ps_buf.at[to, block], pr_buf.at[z, block], p_ss.at[o, block], p_rs.at[o, block],
            dev(s, d, to),
        )

    for o in range(nd):
        block = lax.rem(d + nd - o, nd)
        if o:
            a_copy(o).wait_recv()
        part = jnp.dot(a_buf[block], w_ref[...], preferred_element_type=F32).astype(BF16)
        for zt in range(nz):
            ps_buf[zt, block] = part[zt * sub : (zt + 1) * sub, :]

        @pl.when(jnp.logical_not(below_top))
        def _():
            for oz in range(1, nz):
                p_copy(oz, block).start()

    for o in range(1, nd):
        a_copy(o).wait_send()

    def go(which):
        pl.semaphore_signal(
            go_sem.at[which], inc=1, device_id=dev(jnp.maximum(s - 1, 0), d, z), device_id_type=MESH
        )

    if sections > 1:
        @pl.when(at_top)
        def _():
            go(0)

    scale = 1.0 / math.sqrt(width)
    x_sub = x_ref[pl.ds(sub_start, sub), :].astype(F32)
    radius_sub = jnp.sqrt(jnp.mean(x_sub * x_sub, axis=1, keepdims=True) + eps)
    lifted_sub = (x_sub / radius_sub * gain_ref[...]).astype(BF16)
    table_in = sign_rows(seed_ref[0, 0], 0, width, scale)
    inf_buf[d] = lax.dot_general(lifted_sub, table_in, NT, preferred_element_type=F32)

    def inf_copy(o):
        to = lax.rem(d + o, nd)
        return remote(inf_buf.at[d], inf_buf.at[d], inf_ss.at[o], inf_rs.at[o], dev(s, to, z))

    for o in range(1, nd):
        inf_copy(o).start()


    piece = R * R // nz
    per_seq = nd * sub // SEQS

    def spread():
        for o in range(1, nd):
            inf_copy(o).wait_recv()
        in_feat = inf_buf[...].reshape(nd * sub, R).astype(BF16)
        for zt in range(nz):
            entry = lax.broadcasted_iota(jnp.int32, (R, piece), 1) + zt * piece
            which = lax.broadcasted_iota(jnp.int32, (R, piece), 0)
            pick_in = (entry // R == which).astype(F32).astype(BF16)
            pick_buf[zt] = (entry % R == which).astype(F32).astype(BF16)
            left_buf[zt] = jnp.dot(in_feat, pick_in, preferred_element_type=F32)

    @pl.when(jnp.logical_not(at_top))
    def _():
        spread()

    if sections > 1:
        @pl.when(below_top)
        def _():
            pl.semaphore_wait(go_sem.at[1], 1)
            for o in range(nd):
                block = lax.rem(d + nd - o, nd)
                for oz in range(1, nz):
                    p_copy(oz, block).start()

    table_out = sign_rows(seed_ref[0, 1], d_start, cols, scale)

    def gp_copy(o, block):
        to = lax.rem(z + o, nz)
        return remote(
            gp_buf.at[z, block], gp_buf.at[z, block], gp_ss.at[o, block], gp_rs.at[o, block],
            dev(s, d, to),
        )

    for o in range(nd):
        block = lax.rem(d + nd - o, nd)
        summed = ps_buf[z, block].astype(F32)
        for oz in range(1, nz):
            p_copy(oz, block).wait_recv()
            summed = summed + pr_buf[lax.rem(z + nz - oz, nz), block].astype(F32)
        sig = jax.nn.sigmoid(summed)
        slope = sig * (1.0 + summed * (1.0 - sig))
        sum_buf[block] = summed
        slope_buf[block] = slope

        @pl.when(at_top)
        def _():
            if o:
                og_copy(o).wait_recv()
            else:
                ui_load().wait()
            gp_buf[z, block] = (ui_buf[block].astype(F32) * slope).astype(BF16)
            if sections > 1:
                for oz in range(1, nz):
                    gp_copy(oz, block).start()

    def up_copy(zt, source):
        return remote(
            up_buf.at[pl.ds(zt * sub, sub)], ui_buf.at[source], up_ss.at[zt], up_rs.at[source],
            dev(jnp.maximum(s - 1, 0), z, zt),
        )

    def uii_copy():
        return remote(up_buf, uii_buf, uii_ss.at[0], uii_rs.at[0], dev(jnp.maximum(s - 1, 0), d, z))

    @pl.when(at_top)
    def _():
        uii_load().wait()
        spread()

    @pl.when(jnp.logical_not(at_top))
    def _():
        for source in range(nd):
            up_copy(0, source).wait_recv()
        gp_buf[z] = (ui_buf[...].astype(F32) * slope_buf[...]).astype(BF16)

        @pl.when(lower)
        def _():
            for block in range(nd):
                for oz in range(1, nz):
                    gp_copy(oz, block).start()

    pl.semaphore_wait(far_sem.at[0], column - 1)
    grad_pre = gp_buf[z]
    plane = nd * nz
    mine = d * nz + z

    def dt_copy(o):
        to = lax.rem(mine + o, plane)
        return remote(
            dot_buf.at[mine], dot_buf.at[mine], dt_ss.at[o], dt_rs.at[o],
            dev(s, to // nz, lax.rem(to, nz)),
        )

    @pl.when(lower)
    def _():
        pre = gp_buf[z].astype(F32) * sum_buf[...]
        own_dot = jnp.sum(pre.reshape(nd * sub, cols), axis=1, keepdims=True)
        dot_buf[mine] = jnp.broadcast_to(own_dot, (tok, tok)).T[:8, :]
        for o in range(1, plane):
            dt_copy(o).start()

    out_feat = lax.dot_general(
        grad_pre.reshape(nd * sub, cols), table_out, NT, preferred_element_type=F32
    ).astype(BF16)
    for zt in range(nz):
        product = left_buf[zt] * jnp.dot(out_feat, pick_buf[zt], preferred_element_type=F32)
        for k in range(SEQS):
            g_buf[zt, k : k + 1, :] = jnp.sum(
                product[k * per_seq : (k + 1) * per_seq], axis=0, keepdims=True
            )

    def g_copy(o):
        to = lax.rem(mine + o, plane)
        return remote(
            g_buf.at[lax.rem(to, nz)], gr_buf.at[mine], g_ss.at[o], g_rs.at[o],
            dev(s, to // nz, lax.rem(to, nz)),
        )

    for o in range(1, plane):
        g_copy(o).start()
    gr_buf[mine] = g_buf[z]

    def gn_copy(o):
        to = lax.rem(d + nd - o, nd)
        return remote(gns_buf.at[to], gnr_buf.at[d], gn_ss.at[o], gn_rs.at[o], dev(s, to, z))

    @pl.when(lower)
    def _():
        for o in range(nd):
            block = lax.rem(d + nd - o, nd)
            for oz in range(1, nz):
                gp_copy(oz, block).wait_recv()
            if o == nd - 1:
                for each in range(nd):
                    for oz in range(1, nz):
                        gp_copy(oz, each).wait_send()

                @pl.when(at_top)
                def _():
                    go(1)

            rows = gp_buf[:, block].reshape(tok, cols)
            part = lax.dot_general(rows, w_ref[...], NT, preferred_element_type=F32).astype(BF16)
            if o:
                gns_buf[block] = part
                gn_copy(o).start()
            else:
                gnr_buf[d] = part
        for o in range(1, plane):
            dt_copy(o).wait_recv()
        for zt in range(nz):
            dots = dot_buf[zt]
            for dt in range(1, nd):
                dots = dots + dot_buf[dt * nz + zt]
            turn_buf[...] = jnp.broadcast_to(dots[:1, :] * (1.0 / width), (tok, tok)).T
            mean_buf[zt] = turn_buf[pl.ds(sub_start_d, sub), :]
        for o in range(1, nd):
            gn_copy(o).wait_recv()
        grad_norm = gnr_buf[0].astype(F32)
        for dt in range(1, nd):
            grad_norm = grad_norm + gnr_buf[dt].astype(F32)
        grad_norm = grad_norm.astype(BF16).astype(F32)
        scaled = grad_norm * gain_ref[:, pl.ds(z_start, feat)]
        normed = norm_buf[...]
        rad = rad_buf[:, :1]
        mean_dot = mean_buf[...].reshape(tok, tok)[:, :1]
        if sections > 2:
            @pl.when(jnp.logical_not(at_top))
            def _():
                uii_copy().wait_recv()
        up_buf[...] = (uii_buf[...].astype(F32) + (scaled - normed * mean_dot) / rad).astype(BF16)
        for zt in range(nz):
            up_copy(zt, d).start()
        if sections > 2:
            @pl.when(s > 1)
            def _():
                uii_copy().start()

    for o in range(1, plane):
        g_copy(o).wait_recv()
    grads = gr_buf[0]
    for other in range(1, plane):
        grads = grads + gr_buf[other]
    out_ref[:, :piece] = grads
    queries = q_ref[...]
    high = grads.astype(BF16)
    rest = grads - high.astype(F32)
    middle = rest.astype(BF16)
    low = (rest - middle.astype(F32)).astype(BF16)
    part = lax.dot_general(high, queries, NT, preferred_element_type=F32)
    part = part + lax.dot_general(middle, queries, NT, preferred_element_type=F32)
    part = part + lax.dot_general(low, queries, NT, preferred_element_type=F32)
    sc_buf[here] = part

    def sc_copy(o):
        to = lax.rem(here + o, column)
        return remote(
            sc_buf.at[here], sc_buf.at[here], sc_ss.at[o], sc_rs.at[o],
            dev(to // nz, d, lax.rem(to, nz)),
        )

    for o in range(1, column):
        sc_copy(o).start()

    for o in range(1, nd):
        inf_copy(o).wait_send()
    for block in range(nd):
        for oz in range(1, nz):
            p_copy(oz, block).wait_send()

    @pl.when(at_top)
    def _():
        for o in range(1, nd):
            og_copy(o).wait_send()

    @pl.when(lower)
    def _():
        for o in range(1, plane):
            dt_copy(o).wait_send()
        for o in range(1, nd):
            gn_copy(o).wait_send()
        for zt in range(nz):
            up_copy(zt, d).wait_send()
        if sections > 2:
            @pl.when(s > 1)
            def _():
                uii_copy().wait_send()

    for o in range(1, plane):
        g_copy(o).wait_send()
    for o in range(1, column):
        sc_copy(o).wait_recv()
    scores = sc_buf[0]
    for other in range(1, column):
        scores = scores + sc_buf[other]
    out_ref[:, piece : piece + scores.shape[1]] = scores
    for o in range(1, column):
        sc_copy(o).wait_send()


def body(section_input, weights, gains, proj_seeds, out_grad, query_grads):
    sections = lax.axis_size("section")
    nd = lax.axis_size("dp")
    nz = lax.axis_size("tensor")
    tok, width = section_input.shape[1:]
    feat = weights.shape[1]
    cols = weights.shape[2]
    assert nd == nz and feat == cols
    sub = tok // nz
    piece = R * R // nz
    queries = query_grads.shape[1]
    column = sections * nz
    plane = nd * nz
    vmem = pl.BlockSpec(memory_space=pltpu.VMEM)
    hbm = pl.BlockSpec(memory_space=pl.ANY)
    dma = pltpu.SemaphoreType.DMA
    sems = []
    for shape in ((nd,), (nd,), (nz, nd), (nd,), (nz, nd), (nd,), (plane,)):
        sems += [dma(shape), dma(shape)]
    sems += [dma((nz,)), dma((nd,)), dma((1,)), dma((1,))]
    sems += [dma((plane,)), dma((plane,)), dma((column,)), dma((column,))]
    out = pl.pallas_call(
        functools.partial(kernel, sections, nd, nz),
        out_shape=jax.ShapeDtypeStruct((SEQS, piece + queries), F32),
        in_specs=[hbm, hbm, vmem, pl.BlockSpec(memory_space=pltpu.SMEM), hbm, vmem],
        out_specs=vmem,
        scratch_shapes=[
            pltpu.VMEM((nd, tok, feat), BF16),
            pltpu.VMEM((nd, sub, R), F32),
            pltpu.VMEM((nz, nd, sub, cols), BF16),
            pltpu.VMEM((nz, nd, sub, cols), BF16),
            pltpu.VMEM((nd, sub, cols), F32),
            pltpu.VMEM((nd, sub, cols), BF16),
            pltpu.VMEM((tok, feat), BF16),
            pltpu.VMEM((nz, nd, sub, cols), BF16),
            pltpu.VMEM((nd, tok, feat), BF16),
            pltpu.VMEM((nd, tok, feat), BF16),
            pltpu.VMEM((plane, 8, tok), F32),
            pltpu.VMEM((tok, feat), BF16),
            pltpu.VMEM((nz, SEQS, piece), F32),
            pltpu.VMEM((plane, SEQS, piece), F32),
            pltpu.VMEM((column, SEQS, queries), F32),
            pltpu.VMEM((tok, width), BF16),
            pltpu.VMEM((feat, cols), BF16),
            pltpu.VMEM((nd, sub, cols), F32),
            pltpu.VMEM((tok, feat), F32),
            pltpu.VMEM((tok, 128), F32),
            pltpu.VMEM((tok, tok), F32),
            pltpu.VMEM((nz, sub, tok), F32),
            pltpu.VMEM((nz, tok, piece), F32),
            pltpu.VMEM((nz, R, piece), BF16),
            *sems,
            dma((4,)),
            pltpu.SemaphoreType.REGULAR((2,)),
            pltpu.SemaphoreType.REGULAR((1,)),
        ],
        compiler_params=pltpu.CompilerParams(
            collective_id=0, has_side_effects=True, vmem_limit_bytes=60 * 1024 * 1024
        ),
    )(section_input[0], weights[0], gains, proj_seeds, out_grad, query_grads[0])
    return (out[None, :, :piece], out[:, piece:])


def solution(mesh):
    in_specs = (
        P("section", "dp", None),
        P("section", "tensor", "dp"),
        P("section", None),
        P("section", None),
        P("dp", None),
        P("section", "dp", "tensor"),
    )
    out_specs = (P("section", None, "tensor"), P(None, "dp"))
    return jax.shard_map(body, mesh=mesh, in_specs=in_specs, out_specs=out_specs, check_vma=False)
```

```python
import functools
import math

import jax
import jax.numpy as jnp
from jax import lax
from jax.experimental import pallas as pl
from jax.experimental.pallas import tpu as pltpu
from jax.sharding import PartitionSpec as P

R = 64
SEQS = 2
eps = 1e-05
F32 = jnp.float32
BF16 = jnp.bfloat16
MESH = pl.DeviceIdType.MESH
NT = (((1,), (1,)), ((), ()))


def sign_rows(seed_value, row_start, row_count, scale):
    row_index = lax.broadcasted_iota(jnp.int32, (R, row_count), 1) + row_start
    col_index = lax.broadcasted_iota(jnp.int32, (R, row_count), 0)
    mixing = row_index * 40503 + col_index * 9973 + (seed_value * 7919 + 12345)
    mixing = mixing ^ (mixing >> 13)
    mixing = mixing * 1274126177
    mixing = mixing ^ (mixing >> 16)
    parity = (mixing >> 10) & 1
    return jnp.where(parity == 1, scale, -scale).astype(BF16)


def kernel(
    sections, nd, nz,
    x_hbm, w_hbm, gain_ref, seed_ref, og_ref, q_ref,
    out_ref,
    a_buf, inf_buf, ps_buf, pr_buf, slope_buf, ui_buf, uii_buf, gp_buf,
    gns_buf, gnr_buf, dot_buf, up_buf, g_buf, gr_buf, sc_buf,
    x_ref, w_ref, sum_buf, norm_buf, rad_buf, turn_buf, mean_buf, left_buf, pick_buf,
    a_ss, a_rs, inf_ss, inf_rs, p_ss, p_rs, og_ss, og_rs, gp_ss, gp_rs,
    gn_ss, gn_rs, dt_ss, dt_rs, up_ss, up_rs, uii_ss, uii_rs,
    g_ss, g_rs, sc_ss, sc_rs, in_sem, go_sem, far_sem,
):
    s = lax.axis_index("section")
    d = lax.axis_index("dp")
    z = lax.axis_index("tensor")
    tok, width = x_hbm.shape
    feat = width // nz
    cols = width // nd
    sub = tok // nz
    at_top = s == sections - 1
    below_top = s == sections - 2
    lower = s > 0
    z_start = pl.multiple_of(z * feat, feat)
    d_start = pl.multiple_of(d * cols, cols)
    sub_start = pl.multiple_of(z * sub, sub)
    sub_start_d = pl.multiple_of(d * sub, sub)

    def dev(s_to, d_to, z_to):
        return {"section": s_to, "dp": d_to, "tensor": z_to}

    def remote(src, dst, ss, rs, to):
        return pltpu.make_async_remote_copy(
            src_ref=src, dst_ref=dst, send_sem=ss, recv_sem=rs, device_id=to, device_id_type=MESH
        )

    x_load = pltpu.make_async_copy(x_hbm, x_ref, in_sem.at[0])
    w_load = pltpu.make_async_copy(w_hbm, w_ref, in_sem.at[1])
    x_load.start()
    w_load.start()

    barrier = pltpu.get_barrier_semaphore()
    column = sections * nz
    here = s * nz + z

    def signal_column(sem):
        for o in range(1, column):
            to = lax.rem(here + o, column)
            pl.semaphore_signal(
                sem, inc=1, device_id=dev(to // nz, d, lax.rem(to, nz)), device_id_type=MESH
            )

    for o in range(1, nd):
        pl.semaphore_signal(
            barrier, inc=1, device_id=dev(s, lax.rem(d + o, nd), z), device_id_type=MESH
        )
    signal_column(barrier)

    x_load.wait()
    hidden = x_ref[...].astype(F32)
    radius = jnp.sqrt(jnp.mean(hidden * hidden, axis=1, keepdims=True) + eps)
    gain_z = gain_ref[:, pl.ds(z_start, feat)]
    normed_z = x_ref[:, pl.ds(z_start, feat)].astype(F32) / radius
    norm_buf[...] = normed_z
    rad_buf[...] = jnp.broadcast_to(radius, rad_buf.shape)
    a_buf[d] = (normed_z * gain_z).astype(BF16)

    pl.semaphore_wait(barrier, nd - 1 + column - 1)

    def a_copy(o):
        to = lax.rem(d + o, nd)
        return remote(a_buf.at[d], a_buf.at[d], a_ss.at[o], a_rs.at[o], dev(s, to, z))

    @pl.when(jnp.logical_not(below_top))
    def _():
        for o in range(1, nd):
            a_copy(o).start()

    def og_copy(o):
        to = lax.rem(d + o, nd)
        src = og_ref.at[pl.ds(sub_start, sub), pl.ds(pl.multiple_of(to * cols, cols), cols)]
        return remote(src, ui_buf.at[d], og_ss.at[o], og_rs.at[o], dev(s, to, z))

    def ui_load():
        src = og_ref.at[pl.ds(sub_start, sub), pl.ds(d_start, cols)]
        return pltpu.make_async_copy(src, ui_buf.at[d], in_sem.at[2])

    def uii_load():
        return pltpu.make_async_copy(og_ref.at[:, pl.ds(z_start, feat)], uii_buf, in_sem.at[3])

    @pl.when(at_top)
    def _():
        for o in range(1, nd):
            og_copy(o).start()
        ui_load().start()
        uii_load().start()

    @pl.when(below_top)
    def _():
        pl.semaphore_wait(go_sem.at[0], 1)
        for o in range(1, nd):
            a_copy(o).start()

    signal_column(far_sem.at[0])

    w_load.wait()

    def p_copy(o, block):
        to = lax.rem(z + o, nz)
        return remote(
            ps_buf.at[to, block], pr_buf.at[z, block], p_ss.at[o, block], p_rs.at[o, block],
            dev(s, d, to),
        )

    for o in range(nd):
        block = lax.rem(d + nd - o, nd)
        if o:
            a_copy(o).wait_recv()
        part = jnp.dot(a_buf[block], w_ref[...], preferred_element_type=F32).astype(BF16)
        for zt in range(nz):
            ps_buf[zt, block] = part[zt * sub : (zt + 1) * sub, :]

        @pl.when(jnp.logical_not(below_top))
        def _():
            for oz in range(1, nz):
                p_copy(oz, block).start()

    for o in range(1, nd):
        a_copy(o).wait_send()

    def go(which):
        pl.semaphore_signal(
            go_sem.at[which], inc=1, device_id=dev(jnp.maximum(s - 1, 0), d, z), device_id_type=MESH
        )

    if sections > 1:
        @pl.when(at_top)
        def _():
            go(0)

    scale = 1.0 / math.sqrt(width)
    x_sub = x_ref[pl.ds(sub_start, sub), :].astype(F32)
    radius_sub = jnp.sqrt(jnp.mean(x_sub * x_sub, axis=1, keepdims=True) + eps)
    lifted_sub = (x_sub / radius_sub * gain_ref[...]).astype(BF16)
    table_in = sign_rows(seed_ref[0, 0], 0, width, scale)
    inf_buf[d] = lax.dot_general(lifted_sub, table_in, NT, preferred_element_type=F32)

    def inf_copy(o):
        to = lax.rem(d + o, nd)
        return remote(inf_buf.at[d], inf_buf.at[d], inf_ss.at[o], inf_rs.at[o], dev(s, to, z))

    for o in range(1, nd):
        inf_copy(o).start()


    piece = R * R // nz
    per_seq = nd * sub // SEQS

    def spread():
        for o in range(1, nd):
            inf_copy(o).wait_recv()
        in_feat = inf_buf[...].reshape(nd * sub, R).astype(BF16)
        for zt in range(nz):
            entry = lax.broadcasted_iota(jnp.int32, (R, piece), 1) + zt * piece
            which = lax.broadcasted_iota(jnp.int32, (R, piece), 0)
            pick_in = (entry // R == which).astype(F32).astype(BF16)
            pick_buf[zt] = (entry % R == which).astype(F32).astype(BF16)
            left_buf[zt] = jnp.dot(in_feat, pick_in, preferred_element_type=F32)

    @pl.when(jnp.logical_not(at_top))
    def _():
        spread()

    if sections > 1:
        @pl.when(below_top)
        def _():
            pl.semaphore_wait(go_sem.at[1], 1)
            for o in range(nd):
                block = lax.rem(d + nd - o, nd)
                for oz in range(1, nz):
                    p_copy(oz, block).start()

    table_out = sign_rows(seed_ref[0, 1], d_start, cols, scale)

    def gp_copy(o, block):
        to = lax.rem(z + o, nz)
        return remote(
            gp_buf.at[z, block], gp_buf.at[z, block], gp_ss.at[o, block], gp_rs.at[o, block],
            dev(s, d, to),
        )

    for o in range(nd):
        block = lax.rem(d + nd - o, nd)
        summed = ps_buf[z, block].astype(F32)
        for oz in range(1, nz):
            p_copy(oz, block).wait_recv()
            summed = summed + pr_buf[lax.rem(z + nz - oz, nz), block].astype(F32)
        sig = jax.nn.sigmoid(summed)
        slope = sig * (1.0 + summed * (1.0 - sig))
        sum_buf[block] = summed
        slope_buf[block] = slope

        @pl.when(at_top)
        def _():
            if o:
                og_copy(o).wait_recv()
            else:
                ui_load().wait()
            gp_buf[z, block] = (ui_buf[block].astype(F32) * slope).astype(BF16)
            if sections > 1:
                for oz in range(1, nz):
                    gp_copy(oz, block).start()

    def up_copy(zt, source):
        return remote(
            up_buf.at[pl.ds(zt * sub, sub)], ui_buf.at[source], up_ss.at[zt], up_rs.at[source],
            dev(jnp.maximum(s - 1, 0), z, zt),
        )

    def uii_copy():
        return remote(up_buf, uii_buf, uii_ss.at[0], uii_rs.at[0], dev(jnp.maximum(s - 1, 0), d, z))

    @pl.when(at_top)
    def _():
        uii_load().wait()
        spread()

    @pl.when(jnp.logical_not(at_top))
    def _():
        for source in range(nd):
            up_copy(0, source).wait_recv()
        gp_buf[z] = (ui_buf[...].astype(F32) * slope_buf[...]).astype(BF16)

        @pl.when(lower)
        def _():
            for block in range(nd):
                for oz in range(1, nz):
                    gp_copy(oz, block).start()

    pl.semaphore_wait(far_sem.at[0], column - 1)
    grad_pre = gp_buf[z]
    plane = nd * nz
    mine = d * nz + z

    def dt_copy(o):
        to = lax.rem(mine + o, plane)
        return remote(
            dot_buf.at[mine], dot_buf.at[mine], dt_ss.at[o], dt_rs.at[o],
            dev(s, to // nz, lax.rem(to, nz)),
        )

    @pl.when(lower)
    def _():
        pre = gp_buf[z].astype(F32) * sum_buf[...]
        own_dot = jnp.sum(pre.reshape(nd * sub, cols), axis=1, keepdims=True)
        dot_buf[mine] = jnp.broadcast_to(own_dot, (tok, tok)).T[:8, :]
        for o in range(1, plane):
            dt_copy(o).start()

    out_feat = lax.dot_general(
        grad_pre.reshape(nd * sub, cols), table_out, NT, preferred_element_type=F32
    ).astype(BF16)
    for zt in range(nz):
        product = left_buf[zt] * jnp.dot(out_feat, pick_buf[zt], preferred_element_type=F32)
        for k in range(SEQS):
            g_buf[zt, k : k + 1, :] = jnp.sum(
                product[k * per_seq : (k + 1) * per_seq], axis=0, keepdims=True
            )

    def g_copy(o):
        to = lax.rem(mine + o, plane)
        return remote(
            g_buf.at[lax.rem(to, nz)], gr_buf.at[mine], g_ss.at[o], g_rs.at[o],
            dev(s, to // nz, lax.rem(to, nz)),
        )

    for o in range(1, plane):
        g_copy(o).start()
    gr_buf[mine] = g_buf[z]

    def gn_copy(o):
        to = lax.rem(d + nd - o, nd)
        return remote(gns_buf.at[to], gnr_buf.at[d], gn_ss.at[o], gn_rs.at[o], dev(s, to, z))

    @pl.when(lower)
    def _():
        for o in range(nd):
            block = lax.rem(d + nd - o, nd)
            for oz in range(1, nz):
                gp_copy(oz, block).wait_recv()
            if o == nd - 1:
                for each in range(nd):
                    for oz in range(1, nz):
                        gp_copy(oz, each).wait_send()

                @pl.when(at_top)
                def _():
                    go(1)

            rows = gp_buf[:, block].reshape(tok, cols)
            part = lax.dot_general(rows, w_ref[...], NT, preferred_element_type=F32).astype(BF16)
            if o:
                gns_buf[block] = part
                gn_copy(o).start()
            else:
                gnr_buf[d] = part
        for o in range(1, plane):
            dt_copy(o).wait_recv()
        for zt in range(nz):
            dots = dot_buf[zt]
            for dt in range(1, nd):
                dots = dots + dot_buf[dt * nz + zt]
            turn_buf[...] = jnp.broadcast_to(dots[:1, :] * (1.0 / width), (tok, tok)).T
            mean_buf[zt] = turn_buf[pl.ds(sub_start_d, sub), :]
        for o in range(1, nd):
            gn_copy(o).wait_recv()
        if sections > 2:
            @pl.when(jnp.logical_not(at_top))
            def _():
                uii_copy().wait_recv()
        for zt in range(nz):
            rows = pl.ds(zt * sub, sub)
            grad_norm = gnr_buf[0, rows].astype(F32)
            for dt in range(1, nd):
                grad_norm = grad_norm + gnr_buf[dt, rows].astype(F32)
            scaled = grad_norm.astype(BF16).astype(F32) * gain_ref[:, pl.ds(z_start, feat)]
            change = (scaled - norm_buf[rows] * mean_buf[zt][:, :1]) / rad_buf[rows, :1]
            up_buf[rows] = (uii_buf[rows].astype(F32) + change).astype(BF16)
            up_copy(zt, d).start()
        if sections > 2:
            @pl.when(s > 1)
            def _():
                uii_copy().start()

    for o in range(1, plane):
        g_copy(o).wait_recv()
    grads = gr_buf[0]
    for other in range(1, plane):
        grads = grads + gr_buf[other]
    out_ref[:, :piece] = grads
    queries = q_ref[...]
    high = grads.astype(BF16)
    rest = grads - high.astype(F32)
    middle = rest.astype(BF16)
    low = (rest - middle.astype(F32)).astype(BF16)
    part = lax.dot_general(high, queries, NT, preferred_element_type=F32)
    part = part + lax.dot_general(middle, queries, NT, preferred_element_type=F32)
    part = part + lax.dot_general(low, queries, NT, preferred_element_type=F32)
    sc_buf[here] = part

    def sc_copy(o):
        to = lax.rem(here + o, column)
        return remote(
            sc_buf.at[here], sc_buf.at[here], sc_ss.at[o], sc_rs.at[o],
            dev(to // nz, d, lax.rem(to, nz)),
        )

    for o in range(1, column):
        sc_copy(o).start()

    for o in range(1, nd):
        inf_copy(o).wait_send()
    for block in range(nd):
        for oz in range(1, nz):
            p_copy(oz, block).wait_send()

    @pl.when(at_top)
    def _():
        for o in range(1, nd):
            og_copy(o).wait_send()

    @pl.when(lower)
    def _():
        for o in range(1, plane):
            dt_copy(o).wait_send()
        for o in range(1, nd):
            gn_copy(o).wait_send()
        for zt in range(nz):
            up_copy(zt, d).wait_send()
        if sections > 2:
            @pl.when(s > 1)
            def _():
                uii_copy().wait_send()

    for o in range(1, plane):
        g_copy(o).wait_send()
    for o in range(1, column):
        sc_copy(o).wait_recv()
    scores = sc_buf[0]
    for other in range(1, column):
        scores = scores + sc_buf[other]
    out_ref[:, piece : piece + scores.shape[1]] = scores
    for o in range(1, column):
        sc_copy(o).wait_send()


def part_outputs(both_ref, grads_ref, scores_ref):
    piece = grads_ref.shape[1]
    grads_ref[...] = both_ref[:, :piece]
    scores_ref[...] = both_ref[:, piece : piece + scores_ref.shape[1]]


def body(section_input, weights, gains, proj_seeds, out_grad, query_grads):
    sections = lax.axis_size("section")
    nd = lax.axis_size("dp")
    nz = lax.axis_size("tensor")
    tok, width = section_input.shape[1:]
    feat = weights.shape[1]
    cols = weights.shape[2]
    assert nd == nz and feat == cols
    sub = tok // nz
    piece = R * R // nz
    queries = query_grads.shape[1]
    column = sections * nz
    plane = nd * nz
    vmem = pl.BlockSpec(memory_space=pltpu.VMEM)
    hbm = pl.BlockSpec(memory_space=pl.ANY)
    dma = pltpu.SemaphoreType.DMA
    sems = []
    for shape in ((nd,), (nd,), (nz, nd), (nd,), (nz, nd), (nd,), (plane,)):
        sems += [dma(shape), dma(shape)]
    sems += [dma((nz,)), dma((nd,)), dma((1,)), dma((1,))]
    sems += [dma((plane,)), dma((plane,)), dma((column,)), dma((column,))]
    out = pl.pallas_call(
        functools.partial(kernel, sections, nd, nz),
        out_shape=jax.ShapeDtypeStruct((SEQS, piece + queries), F32),
        in_specs=[hbm, hbm, vmem, pl.BlockSpec(memory_space=pltpu.SMEM), hbm, vmem],
        out_specs=vmem,
        scratch_shapes=[
            pltpu.VMEM((nd, tok, feat), BF16),
            pltpu.VMEM((nd, sub, R), F32),
            pltpu.VMEM((nz, nd, sub, cols), BF16),
            pltpu.VMEM((nz, nd, sub, cols), BF16),
            pltpu.VMEM((nd, sub, cols), F32),
            pltpu.VMEM((nd, sub, cols), BF16),
            pltpu.VMEM((tok, feat), BF16),
            pltpu.VMEM((nz, nd, sub, cols), BF16),
            pltpu.VMEM((nd, tok, feat), BF16),
            pltpu.VMEM((nd, tok, feat), BF16),
            pltpu.VMEM((plane, 8, tok), F32),
            pltpu.VMEM((tok, feat), BF16),
            pltpu.VMEM((nz, SEQS, piece), F32),
            pltpu.VMEM((plane, SEQS, piece), F32),
            pltpu.VMEM((column, SEQS, queries), F32),
            pltpu.VMEM((tok, width), BF16),
            pltpu.VMEM((feat, cols), BF16),
            pltpu.VMEM((nd, sub, cols), F32),
            pltpu.VMEM((tok, feat), F32),
            pltpu.VMEM((tok, 128), F32),
            pltpu.VMEM((tok, tok), F32),
            pltpu.VMEM((nz, sub, tok), F32),
            pltpu.VMEM((nz, tok, piece), F32),
            pltpu.VMEM((nz, R, piece), BF16),
            *sems,
            dma((4,)),
            pltpu.SemaphoreType.REGULAR((2,)),
            pltpu.SemaphoreType.REGULAR((1,)),
        ],
        compiler_params=pltpu.CompilerParams(
            collective_id=0, has_side_effects=True, vmem_limit_bytes=60 * 1024 * 1024
        ),
    )(section_input[0], weights[0], gains, proj_seeds, out_grad, query_grads[0])
    grads, scores = pl.pallas_call(
        part_outputs,
        out_shape=(
            jax.ShapeDtypeStruct((SEQS, piece), F32),
            jax.ShapeDtypeStruct((SEQS, queries), F32),
        ),
        in_specs=[vmem],
        out_specs=(vmem, vmem),
    )(out)
    return (grads[None], scores)


def solution(mesh):
    in_specs = (
        P("section", "dp", None),
        P("section", "tensor", "dp"),
        P("section", None),
        P("section", None),
        P("dp", None),
        P("section", "dp", "tensor"),
    )
    out_specs = (P("section", None, "tensor"), P(None, "dp"))
    return jax.shard_map(body, mesh=mesh, in_specs=in_specs, out_specs=out_specs, check_vma=False)
```
